128 devices in a mesh: segment: 4 (over x), th: 4 (over y_lo, core), tw: 8 (over z, y_hi).
Axes of the slice: x: 4, y: 4 (y_hi: 2, y_lo: 2; y = y_hi * 2 + y_lo), z: 4, core: 2. Of those that a mesh axis runs over, the one named last changes fastest.
Arguments:
- tokens: bfloat16 [16, 16, 48, 2048], P(None, 'th', 'tw'), may hold values from -6 to 6
- frame_order: int32 [16], replicated, may hold values from 0 to 15, each once
- tile_pattern: int32 [4, 8, 9], P('th', 'tw'), may hold values from 0 to 1, as said below
- qkv_weight: bfloat16 [4, 2048, 4608], P('segment'), may hold values from -0.125 to 0.125
- out_weight: bfloat16 [4, 1536, 2048], P('segment'), may hold values from -0.15625 to 0.15625
- modulation: float32 [4, 3, 2048], P('segment'), may hold values from -4 to 4
Outputs:
- hidden_states: bfloat16 [16, 16, 48, 2048], P('segment', 'th', 'tw')
The draws below stay inside these ranges and needn't reach their ends.
Inputs may be any that keep to these rules, and one draw needn't show every extreme that they name: `tile_pattern`: each entry is 0 or 1; entry 4 (the tile itself) is 1 for every tile.
All inputs are finite; a program needn't handle non-finite values.
Results may differ from the reference program's by a relative error of at most 0.01.
Values may be sent and summed in bfloat16 or wider, within the bound.
A program may use at most 128 MiB of HBM per device.

```python
import math
import jax
import jax.numpy as jnp
from jax import lax

D = 2048
HEADS = 12
HEAD = 128
TILE_H = 4
TILE_W = 6
HALO = 1
FRAME_PATCH = 4
PATCHES = 4
SECTIONS = 4
FRAMES = 16
TILES_H = 4
TILES_W = 8
GRID_H = 16
GRID_W = 48


def draw_tile_pattern(key, part):
    draws = jax.random.randint(key, (TILES_H, TILES_W, 9), 0, 4)
    flags = (draws > 0).astype(jnp.int32)
    centre = jnp.arange(9) == 4
    return jnp.where(centre[None, None, :], 1, flags).astype(jnp.int32)


def levels(stream_key, extent, cuts, low, top_value):
    loudness, own = 1.0, jax.random.fold_in(stream_key, 6)
    for position, blocks in cuts:
        steps = jnp.exp(jax.random.uniform(jax.random.fold_in(own, position), (blocks,), jnp.float32, low / len(cuts), top_value / len(cuts)))
        loudness = loudness * jnp.repeat(steps, extent[position] // blocks).reshape([-1 if axis == position else 1 for axis in range(len(extent))])
    return loudness


def bell_draw(own_key, extent, spread, bound, cuts=(), kind=jnp.bfloat16):
    level = levels(own_key, extent, cuts, -0.22, 0.18) if cuts else 1.0
    drawn = jax.random.normal(own_key, extent, jnp.float32) * spread * level
    return jnp.minimum(jnp.maximum(drawn, -bound), bound).astype(kind)


def setup_inputs(seed: int = 0) -> dict:
    seeds = jax.random.split(jax.random.key(seed), 7)
    tokens = bell_draw(seeds[0], (FRAMES, GRID_H, GRID_W, D), 1.0, 6.0, ((1, 4), (2, 8)))
    frame_order = jax.random.permutation(seeds[1], FRAMES).astype(jnp.int32)
    tile_pattern = draw_tile_pattern(jax.random.fold_in(seeds[6], 71), 0)
    qkv_weight = bell_draw(seeds[3], (SECTIONS, D, 3 * HEADS * HEAD), D ** -0.5, 0.125, ((0, 4),))
    out_weight = bell_draw(seeds[4], (SECTIONS, HEADS * HEAD, D), (HEADS * HEAD) ** -0.5, 0.15625, ((0, 4),))
    modulation = bell_draw(seeds[5], (SECTIONS, 3, D), 1.0, 4.0, ((0, 4),), jnp.float32)
    return dict(tokens=tokens, frame_order=frame_order, tile_pattern=tile_pattern, qkv_weight=qkv_weight, out_weight=out_weight, modulation=modulation)


def modulate(hidden, shift_row, scale_row):
    values = hidden.astype(jnp.float32)
    average = lax.optimization_barrier(jnp.mean(values, axis=-1, keepdims=True))
    centred = values - average
    variance = lax.optimization_barrier(jnp.mean(centred * centred, axis=-1, keepdims=True))
    normed = centred * lax.rsqrt(variance + 1e-06)
    return (normed * (1.0 + scale_row) + shift_row).astype(jnp.bfloat16)

def head_norm(values):
    shaped = values.reshape(values.shape[:-1] + (HEADS, HEAD))
    mean_square = lax.optimization_barrier(jnp.mean(shaped * shaped, axis=-1, keepdims=True))
    return (shaped * lax.rsqrt(mean_square + 1e-06)).reshape(values.shape).astype(jnp.bfloat16)

def block_ids(tile_h, tile_w, reach):
    row_range = jnp.arange(tile_h + 2 * reach).astype(jnp.int32)
    col_range = jnp.arange(tile_w + 2 * reach).astype(jnp.int32)
    row_part = (row_range >= reach).astype(jnp.int32) + (row_range >= tile_h + reach).astype(jnp.int32)
    col_part = (col_range >= reach).astype(jnp.int32) + (col_range >= tile_w + reach).astype(jnp.int32)
    return row_part[:, None] * 3 + col_part[None, :]

def attend(queries, key_rows, value_rows, allowed):
    group_count, query_count, inner_width = queries.shape
    key_count = key_rows.shape[1]
    query_heads = queries.reshape(group_count, query_count, HEADS, HEAD).astype(jnp.float32)
    key_heads = key_rows.reshape(group_count, key_count, HEADS, HEAD).astype(jnp.float32)
    value_heads = value_rows.reshape(group_count, key_count, HEADS, HEAD).astype(jnp.float32)
    scores = jnp.einsum('gqhd,gkhd->ghqk', query_heads, key_heads) * (1.0 / math.sqrt(HEAD))
    weighted = jnp.exp(scores) * allowed
    softmax_w = (weighted / lax.optimization_barrier(jnp.sum(weighted, axis=-1, keepdims=True))).astype(jnp.bfloat16)
    attended = jnp.einsum('ghqk,gkhd->gqhd', softmax_w.astype(jnp.float32), value_heads)
    return attended.reshape(group_count, query_count, inner_width).astype(jnp.bfloat16)

def section(hidden, qkv_w, out_w, modulation, tile_pattern):
    inner_width = HEADS * HEAD
    modded = modulate(hidden, modulation[0], modulation[1])
    projected = jnp.dot(modded.reshape(-1, D), qkv_w, preferred_element_type=jnp.float32)
    grid_shape = (PATCHES, FRAME_PATCH, GRID_H, GRID_W, inner_width)
    queries = head_norm(projected[:, :inner_width]).reshape(grid_shape)
    key_rows = head_norm(projected[:, inner_width:2 * inner_width]).reshape(grid_shape)
    value_rows = projected[:, 2 * inner_width:].astype(jnp.bfloat16).reshape(grid_shape)
    padding = ((0, 0), (0, 0), (HALO, HALO), (HALO, HALO), (0, 0))
    key_pad = jnp.pad(key_rows, padding)
    value_pad = jnp.pad(value_rows, padding)
    inside = jnp.pad(jnp.ones((GRID_H, GRID_W), jnp.float32), ((HALO, HALO), (HALO, HALO)))
    ext_rows = TILE_H + 2 * HALO
    ext_cols = TILE_W + 2 * HALO
    block_map = block_ids(TILE_H, TILE_W, HALO)
    nine = jnp.arange(9).astype(jnp.int32)

    def one_tile(tile_index):
        tile_row = tile_index // TILES_W
        tile_col = tile_index % TILES_W
        row_start = (tile_row * TILE_H).astype(jnp.int32)
        col_start = (tile_col * TILE_W).astype(jnp.int32)
        anchor = jnp.zeros((), jnp.int32)
        query_tile = lax.dynamic_slice(queries, (anchor, anchor, row_start, col_start, anchor), (PATCHES, FRAME_PATCH, TILE_H, TILE_W, inner_width))
        key_tile = lax.dynamic_slice(key_pad, (anchor, anchor, row_start, col_start, anchor), (PATCHES, FRAME_PATCH, ext_rows, ext_cols, inner_width))
        value_tile = lax.dynamic_slice(value_pad, (anchor, anchor, row_start, col_start, anchor), (PATCHES, FRAME_PATCH, ext_rows, ext_cols, inner_width))
        inside_tile = lax.dynamic_slice(inside, (row_start, col_start), (ext_rows, ext_cols))
        tile_flags = tile_pattern[tile_row, tile_col]
        chosen = lax.optimization_barrier(jnp.sum(jnp.where(block_map[:, :, None] == nine[None, None, :], tile_flags[None, None, :], 0), axis=-1))
        allowed_grid = inside_tile * chosen.astype(jnp.float32)
        allowed = jnp.broadcast_to(allowed_grid[None], (FRAME_PATCH, ext_rows, ext_cols)).reshape(-1)
        return attend(query_tile.reshape(PATCHES, -1, inner_width), key_tile.reshape(PATCHES, -1, inner_width), value_tile.reshape(PATCHES, -1, inner_width), allowed)
    tile_out = lax.map(one_tile, jnp.arange(TILES_H * TILES_W).astype(jnp.int32))
    tile_out = tile_out.reshape(TILES_H, TILES_W, PATCHES, FRAME_PATCH, TILE_H, TILE_W, inner_width)
    attended = tile_out.transpose(2, 3, 0, 4, 1, 5, 6).reshape(-1, inner_width)
    projected_out = jnp.dot(attended, out_w, preferred_element_type=jnp.float32)
    updated = hidden.astype(jnp.float32).reshape(-1, D) + modulation[2] * projected_out
    return updated.astype(jnp.bfloat16).reshape(hidden.shape)

def reference(tokens, frame_order, tile_pattern, qkv_weight, out_weight, modulation):
    ordered = jnp.take(tokens, frame_order, axis=0)
    hidden = ordered.reshape(PATCHES, FRAME_PATCH, GRID_H, GRID_W, D)
    for section_id in reversed(range(SECTIONS)):
        hidden = section(hidden, qkv_weight[section_id], out_weight[section_id], modulation[section_id], tile_pattern)
    return hidden.reshape(FRAMES, GRID_H, GRID_W, D)
```

```python
import functools
import math

import jax
import jax.numpy as jnp
from jax import lax
from jax.experimental import pallas as pl
from jax.experimental.pallas import tpu as pltpu
from jax.sharding import PartitionSpec as P

HEAD = 128
LANE = 128
FP = 4
MESH = pl.DeviceIdType.MESH
DIRS = [(i, j) for i in (-1, 0, 1) for j in (-1, 0, 1) if (i, j) != (0, 0)]


def span(step, length):
    if step == 0:
        return (0, length), (1, length)
    if step < 0:
        return (0, 1), (length + 1, 1)
    return (length - 1, 1), (0, 1)


def kernel(
    sizes,
    order_ref,
    pattern_ref,
    tokens_hbm,
    wqkv_hbm,
    wout_hbm,
    mod_hbm,
    out_ref,
    wqkv,
    wout,
    mod,
    tok,
    ext,
    outgo,
    fin,
    xs,
    xm,
    q_s,
    k_s,
    v_s,
    att,
    allow,
    wsem,
    own_recv,
    halo_recv,
    own_send,
    halo_send,
    fin_recv,
):
    n_seg, n_th, n_tw, th_len, tw_len, width, inner = sizes
    heads = inner // HEAD
    blocks = width // LANE
    own_n = FP * th_len * tw_len
    ring_n = 2 * (tw_len + 2) + 2 * th_len
    halo_n = FP * ring_n
    patches = n_seg
    seg = lax.axis_index("segment")
    a = lax.axis_index("th")
    b = lax.axis_index("tw")

    qkv_cols = 512
    n_qkv = 3 * inner // qkv_cols
    out_cols = 512
    n_out = width // out_cols

    def wq_copy(i):
        cols = pl.ds(i * qkv_cols, qkv_cols)
        return pltpu.make_async_copy(wqkv_hbm.at[0, :, cols], wqkv.at[:, cols], wsem.at[i])

    def wo_copy(i):
        cols = pl.ds(i * out_cols, out_cols)
        return pltpu.make_async_copy(wout_hbm.at[0, :, cols], wout.at[:, cols], wsem.at[n_qkv + i])

    mod_copy = pltpu.make_async_copy(mod_hbm.at[0], mod, wsem.at[n_qkv + n_out])
    tok_copy = pltpu.make_async_copy(tokens_hbm, tok, wsem.at[n_qkv + n_out + 1])
    mod_copy.start()

    @pl.when(seg == n_seg - 1)
    def _():
        tok_copy.start()

    for i in range(n_qkv):
        wq_copy(i).start()
    for i in range(n_out):
        wo_copy(i).start()

    @pl.loop(0, patches)
    def _(k):
        @pl.loop(0, FP)
        def _(f):
            ext[k, f] = jnp.zeros(ext.shape[2:], ext.dtype)

    barrier = pltpu.get_barrier_semaphore()
    for s in range(1, n_seg):
        other = lax.rem(seg + s, n_seg)
        pl.semaphore_signal(barrier, inc=1, device_id=(other, a, b), device_id_type=MESH)

    def has(da, db):
        ok = None
        for pos, step, count in ((a, da, n_th), (b, db, n_tw)):
            if step == 0:
                continue
            here = pos > 0 if step < 0 else pos < count - 1
            ok = here if ok is None else jnp.logical_and(ok, here)
        return ok

    for da, db in DIRS:

        @pl.when(has(da, db))
        def _():
            pl.semaphore_signal(
                barrier, inc=1, device_id=(seg, a + da, b + db), device_id_type=MESH
            )

    near_rows = 1 + (a > 0).astype(jnp.int32) + (a < n_th - 1).astype(jnp.int32)
    near_cols = 1 + (b > 0).astype(jnp.int32) + (b < n_tw - 1).astype(jnp.int32)
    pl.semaphore_wait(barrier, n_seg - 2 + near_rows * near_cols)

    lane = lax.broadcasted_iota(jnp.int32, (1, own_n + halo_n), 1)
    u = lane - own_n
    for f in range(1, FP):
        u = jnp.where(lane >= own_n + f * ring_n, lane - own_n - f * ring_n, u)
    code = jnp.where(lane < own_n, 4, 0)
    wide = tw_len + 2
    for r, base in ((0, 0), (2, wide)):
        for i in range(wide):
            j = 0 if i == 0 else (2 if i == wide - 1 else 1)
            code = jnp.where((lane >= own_n) & (u == base + i), 3 * r + j, code)
    left = 2 * wide
    code = jnp.where((lane >= own_n) & (u >= left) & (u < left + th_len), 3, code)
    code = jnp.where((lane >= own_n) & (u >= left + th_len), 5, code)
    allowed = jnp.zeros((1, own_n + halo_n), jnp.float32)
    for i in range(3):
        for j in range(3):
            flag = pattern_ref[0, 0, 3 * i + j].astype(jnp.float32)
            if (i, j) != (1, 1):
                flag = flag * has(i - 1, j - 1).astype(jnp.float32)
            allowed = jnp.where(code == 3 * i + j, flag, allowed)
    allow[...] = allowed

    mod_copy.wait()

    @pl.when(seg == n_seg - 1)
    def _():
        tok_copy.wait()

    own_rows, own_cols = pl.ds(1, th_len), pl.ds(1, tw_len)

    def own_copy(k, target, dst, sem):
        return pltpu.make_async_remote_copy(
            src_ref=outgo.at[k],
            dst_ref=dst,
            send_sem=own_send.at[k],
            recv_sem=sem,
            device_id=(target, a, b),
            device_id_type=MESH,
        )

    def next_copy(k):
        return own_copy(k, jnp.maximum(seg - 1, 0), ext.at[k, :, own_rows, own_cols], own_recv.at[k])

    def fin_copy(k):
        return own_copy(k, lax.rem(k + 1, n_seg), fin, fin_recv)

    def halo_copy(k, d):
        da, db = DIRS[d]
        (r0, rn), (rt, _) = span(da, th_len)
        (c0, cn), (ct, _) = span(db, tw_len)
        return pltpu.make_async_remote_copy(
            src_ref=ext.at[k, :, pl.ds(1 + r0, rn), pl.ds(1 + c0, cn)],
            dst_ref=ext.at[k, :, pl.ds(rt, rn), pl.ds(ct, cn)],
            send_sem=halo_send.at[k, d],
            recv_sem=halo_recv.at[k, d],
            device_id=(seg, a + da, b + db),
            device_id_type=MESH,
        )

    def modulate(base):
        @pl.loop(0, own_n // 16)
        def _(g):
            start = (base + g * 16) * blocks
            cols = [xs[pl.ds(start + j, 16, stride=blocks), :] for j in range(blocks)]
            total = cols[0]
            for j in range(1, blocks):
                total = total + cols[j]
            mean = jnp.sum(total, axis=-1, keepdims=True) * (1.0 / width)
            cols = [c - mean for c in cols]
            total = cols[0] * cols[0]
            for j in range(1, blocks):
                total = total + cols[j] * cols[j]
            var = jnp.sum(total, axis=-1, keepdims=True) * (1.0 / width)
            scale = lax.rsqrt(var + 1e-06)
            rows = pl.ds(pl.multiple_of(g * 16, 16), 16)
            for j in range(blocks):
                lanes = pl.ds(j * LANE, LANE)
                value = cols[j] * scale * (1.0 + mod[1:2, lanes]) + mod[0:1, lanes]
                xm[rows, lanes] = value.astype(jnp.bfloat16)

    def project(k, first_col, dst, row0, norm):
        for i in range(inner // qkv_cols):
            chunk = first_col // qkv_cols + i

            @pl.when(k == 0)
            def _():
                wq_copy(chunk).wait()

            cols = pl.ds(chunk * qkv_cols, qkv_cols)
            p = jnp.dot(xm[...], wqkv[:, cols], preferred_element_type=jnp.float32)
            for h in range(qkv_cols // HEAD):
                ph = p[:, h * HEAD : (h + 1) * HEAD]
                if norm:
                    ms = jnp.sum(ph * ph, axis=-1, keepdims=True) * (1.0 / HEAD)
                    ph = ph * lax.rsqrt(ms + 1e-06)
                dst[pl.ds(row0, own_n), pl.ds(i * qkv_cols + h * HEAD, HEAD)] = ph.astype(
                    jnp.bfloat16
                )

    @pl.loop(0, patches)
    def _(k):
        @pl.when(seg == n_seg - 1)
        def _():
            patch = lax.rem(k + 1, n_seg)

            @pl.loop(0, FP)
            def _(f):
                frame = order_ref[patch * FP + f]
                for r in range(th_len):
                    x = tok[frame, r].astype(jnp.float32)
                    base = (f * th_len + r) * tw_len * blocks
                    for j in range(blocks):
                        xs[pl.ds(base + j, tw_len, stride=blocks), :] = x[
                            :, j * LANE : (j + 1) * LANE
                        ]
                for r in range(th_len):
                    base = (f * th_len + r) * tw_len * blocks
                    y = xs[pl.ds(base, tw_len * blocks), :]
                    ext[k, f, 1 + r, 1 : 1 + tw_len] = y.astype(jnp.bfloat16).reshape(
                        tw_len, blocks, LANE
                    )

        @pl.when(seg < n_seg - 1)
        def _():
            next_copy(k).wait_recv()

        for d, (da, db) in enumerate(DIRS):

            @pl.when(has(da, db))
            def _():
                halo_copy(k, d).start()

        @pl.when(seg < n_seg - 1)
        def _():
            @pl.loop(0, FP)
            def _(f):
                for r in range(th_len):
                    y = ext[k, f, 1 + r, 1 : 1 + tw_len]
                    base = (f * th_len + r) * tw_len * blocks
                    xs[pl.ds(base, tw_len * blocks), :] = y.reshape(
                        tw_len * blocks, LANE
                    ).astype(jnp.float32)

        modulate(0)
        project(k, 0, q_s, 0, True)
        project(k, inner, k_s, 0, True)
        project(k, 2 * inner, v_s, 0, False)

        for d, (da, db) in enumerate(DIRS):

            @pl.when(has(-da, -db))
            def _():
                halo_copy(k, d).wait_recv()

        @pl.loop(0, FP)
        def _(f):
            base = (own_n + f * ring_n) * blocks
            for r in (0, th_len + 1):
                y = ext[k, f, r].reshape(wide * blocks, LANE)
                xs[pl.ds(base, wide * blocks), :] = y.astype(jnp.float32)
                base = base + wide * blocks
            for c in (0, tw_len + 1):
                for r in range(th_len):
                    xs[pl.ds(base, blocks), :] = ext[k, f, 1 + r, c].astype(jnp.float32)
                    base = base + blocks

        modulate(own_n)
        project(-1, inner, k_s, own_n, True)
        project(-1, 2 * inner, v_s, own_n, False)

        allowed = allow[...]
        for h in range(heads):
            lanes = pl.ds(h * HEAD, HEAD)
            s = lax.dot_general(
                q_s[:, lanes],
                k_s[:, lanes],
                (((1,), (1,)), ((), ())),
                preferred_element_type=jnp.float32,
            )
            e = jnp.exp(s * (1.0 / math.sqrt(HEAD))) * allowed
            total = jnp.sum(e, axis=-1, keepdims=True)
            o = jnp.dot(
                e.astype(jnp.bfloat16), v_s[:, lanes], preferred_element_type=jnp.float32
            )
            att[:, lanes] = (o / total).astype(jnp.bfloat16)

        for i in range(n_out):

            @pl.when(k == 0)
            def _():
                wo_copy(i).wait()

            acc = jnp.dot(
                att[...], wout[:, pl.ds(i * out_cols, out_cols)], preferred_element_type=jnp.float32
            )
            for j in range(out_cols // LANE):
                block = i * (out_cols // LANE) + j
                rows = pl.ds(block, own_n, stride=blocks)
                gate = mod[2:3, pl.ds(block * LANE, LANE)]
                xs[rows, :] = xs[rows, :] + gate * acc[:, j * LANE : (j + 1) * LANE]

        @pl.loop(0, FP)
        def _(f):
            for r in range(th_len):
                base = (f * th_len + r) * tw_len * blocks
                y = xs[pl.ds(base, tw_len * blocks), :]
                outgo[k, f, r] = y.astype(jnp.bfloat16).reshape(tw_len, blocks, LANE)

        @pl.when(seg > 0)
        def _():
            next_copy(k).start()

        @pl.when(jnp.logical_and(seg == 0, k < patches - 1))
        def _():
            fin_copy(k).start()

    def emit(read):
        @pl.loop(0, FP)
        def _(f):
            for r in range(th_len):
                y = read(f, r).reshape(tw_len * blocks, LANE).astype(jnp.float32)
                base = (f * th_len + r) * tw_len * blocks
                xs[pl.ds(base, tw_len * blocks), :] = y
            for r in range(th_len):
                base = (f * th_len + r) * tw_len * blocks
                for j in range(blocks):
                    out_ref[f, r, :, pl.ds(j * LANE, LANE)] = xs[
                        pl.ds(base + j, tw_len, stride=blocks), :
                    ].astype(jnp.bfloat16)

    @pl.when(seg == 0)
    def _():
        emit(lambda f, r: outgo[patches - 1, f, r])

    @pl.when(seg > 0)
    def _():
        fin_copy(0).wait_recv()
        emit(lambda f, r: fin[f, r])

    @pl.loop(0, patches)
    def _(k):
        @pl.when(jnp.logical_or(seg > 0, k < patches - 1))
        def _():
            next_copy(k).wait_send()

        for d, (da, db) in enumerate(DIRS):

            @pl.when(has(da, db))
            def _():
                halo_copy(k, d).wait_send()


def solution(mesh):
    n_seg, n_th, n_tw = (mesh.shape[name] for name in ("segment", "th", "tw"))

    def on_device(tokens, frame_order, tile_pattern, qkv_weight, out_weight, modulation):
        frames, th_len, tw_len, width = tokens.shape
        inner = out_weight.shape[1]
        blocks = width // LANE
        own_n = FP * th_len * tw_len
        halo_n = FP * (2 * (tw_len + 2) + 2 * th_len)
        all_n = own_n + halo_n
        assert halo_n == own_n and n_seg * FP == frames
        sizes = (n_seg, n_th, n_tw, th_len, tw_len, width, inner)
        bf16, f32 = jnp.bfloat16, jnp.float32
        smem = pl.BlockSpec(memory_space=pltpu.SMEM)
        hbm = pl.BlockSpec(memory_space=pl.ANY)
        dma = pltpu.SemaphoreType.DMA
        return pl.pallas_call(
            functools.partial(kernel, sizes),
            out_shape=jax.ShapeDtypeStruct((FP, th_len, tw_len, width), bf16),
            in_specs=[smem, smem, hbm, hbm, hbm, hbm],
            out_specs=pl.BlockSpec(memory_space=pltpu.VMEM),
            scratch_shapes=[
                pltpu.VMEM((width, 3 * inner), bf16),
                pltpu.VMEM((inner, width), bf16),
                pltpu.VMEM((3, width), f32),
                pltpu.VMEM((frames, th_len, tw_len, width), bf16),
                pltpu.VMEM((n_seg, FP, th_len + 2, tw_len + 2, blocks, LANE), bf16),
                pltpu.VMEM((n_seg, FP, th_len, tw_len, blocks, LANE), bf16),
                pltpu.VMEM((FP, th_len, tw_len, blocks, LANE), bf16),
                pltpu.VMEM((all_n * blocks, LANE), f32),
                pltpu.VMEM((own_n, width), bf16),
                pltpu.VMEM((own_n, inner), bf16),
                pltpu.VMEM((all_n, inner), bf16),
                pltpu.VMEM((all_n, inner), bf16),
                pltpu.VMEM((own_n, inner), bf16),
                pltpu.VMEM((1, all_n), f32),
                dma((3 * inner // 512 + width // 512 + 2,)),
                dma((n_seg,)),
                dma((n_seg, 8)),
                dma((n_seg,)),
                dma((n_seg, 8)),
                dma,
            ],
            compiler_params=pltpu.CompilerParams(
                collective_id=0, has_side_effects=True, vmem_limit_bytes=60 * 1024 * 1024
            ),
            name="sections",
        )(frame_order, tile_pattern, tokens, qkv_weight, out_weight, modulation)

    in_specs = (
        P(None, "th", "tw", None),
        P(),
        P("th", "tw", None),
        P("segment", None, None),
        P("segment", None, None),
        P("segment", None, None),
    )
    out_specs = P("segment", "th", "tw", None)
    return jax.shard_map(
        on_device, mesh=mesh, in_specs=in_specs, out_specs=out_specs, check_vma=False
    )
```

```python
import functools
import math

import jax
import jax.numpy as jnp
from jax import lax
from jax.experimental import pallas as pl
from jax.experimental.pallas import tpu as pltpu
from jax.sharding import PartitionSpec as P

HEAD = 128
LANE = 128
FP = 4
UNROLL = 3
MESH = pl.DeviceIdType.MESH
DIRS = [(i, j) for i in (-1, 0, 1) for j in (-1, 0, 1) if (i, j) != (0, 0)]


def span(step, length):
    if step == 0:
        return (0, length), (1, length)
    if step < 0:
        return (0, 1), (length + 1, 1)
    return (length - 1, 1), (0, 1)


def kernel(
    sizes,
    order_ref,
    pattern_ref,
    tokens_hbm,
    wqkv_hbm,
    wout_hbm,
    mod_hbm,
    out_ref,
    wqkv,
    wout,
    mod,
    tok,
    ext,
    outgo,
    fin,
    xs,
    xm,
    q_s,
    k_s,
    v_s,
    att,
    allow,
    wsem,
    own_recv,
    halo_recv,
    own_send,
    halo_send,
    fin_recv,
):
    n_seg, n_th, n_tw, th_len, tw_len, width, inner = sizes
    heads = inner // HEAD
    blocks = width // LANE
    own_n = FP * th_len * tw_len
    ring_n = 2 * (tw_len + 2) + 2 * th_len
    halo_n = FP * ring_n
    patches = n_seg
    seg = lax.axis_index("segment")
    a = lax.axis_index("th")
    b = lax.axis_index("tw")

    qkv_cols = 512
    n_qkv = 3 * inner // qkv_cols
    out_cols = 512
    n_out = width // out_cols

    def wq_copy(i):
        cols = pl.ds(i * qkv_cols, qkv_cols)
        return pltpu.make_async_copy(wqkv_hbm.at[0, :, cols], wqkv.at[:, cols], wsem.at[i])

    def wo_copy(i):
        cols = pl.ds(i * out_cols, out_cols)
        return pltpu.make_async_copy(wout_hbm.at[0, :, cols], wout.at[:, cols], wsem.at[n_qkv + i])

    mod_copy = pltpu.make_async_copy(mod_hbm.at[:, 0], mod, wsem.at[n_qkv + n_out])
    tok_copy = pltpu.make_async_copy(tokens_hbm, tok, wsem.at[n_qkv + n_out + 1])
    mod_copy.start()

    @pl.when(seg == n_seg - 1)
    def _():
        tok_copy.start()

    for i in range(n_qkv):
        wq_copy(i).start()
    for i in range(n_out):
        wo_copy(i).start()

    row_cells = (tw_len + 2, blocks, LANE)
    for edge, at in ((a == 0, 0), (a == n_th - 1, th_len + 1)):

        @pl.when(edge)
        def _():
            @pl.loop(0, patches * FP)
            def _(i):
                ext[i // FP, i % FP, at] = jnp.zeros(row_cells, ext.dtype)

    for edge, at in ((b == 0, 0), (b == n_tw - 1, tw_len + 1)):

        @pl.when(edge)
        def _():
            @pl.loop(0, patches * FP)
            def _(i):
                for r in range(th_len + 2):
                    ext[i // FP, i % FP, r, at] = jnp.zeros((blocks, LANE), ext.dtype)

    barrier = pltpu.get_barrier_semaphore()
    for s in range(1, n_seg):
        other = lax.rem(seg + s, n_seg)
        pl.semaphore_signal(barrier, inc=1, device_id=(other, a, b), device_id_type=MESH)

    def has(da, db):
        ok = None
        for pos, step, count in ((a, da, n_th), (b, db, n_tw)):
            if step == 0:
                continue
            here = pos > 0 if step < 0 else pos < count - 1
            ok = here if ok is None else jnp.logical_and(ok, here)
        return ok

    for da, db in DIRS:

        @pl.when(has(da, db))
        def _():
            pl.semaphore_signal(
                barrier, inc=1, device_id=(seg, a + da, b + db), device_id_type=MESH
            )

    near_rows = 1 + (a > 0).astype(jnp.int32) + (a < n_th - 1).astype(jnp.int32)
    near_cols = 1 + (b > 0).astype(jnp.int32) + (b < n_tw - 1).astype(jnp.int32)
    pl.semaphore_wait(barrier, n_seg - 2 + near_rows * near_cols)

    lane = lax.broadcasted_iota(jnp.int32, (1, own_n + halo_n), 1)
    u = lane - own_n
    for f in range(1, FP):
        u = jnp.where(lane >= own_n + f * ring_n, lane - own_n - f * ring_n, u)
    code = jnp.where(lane < own_n, 4, 0)
    wide = tw_len + 2
    for r, base in ((0, 0), (2, wide)):
        for i in range(wide):
            j = 0 if i == 0 else (2 if i == wide - 1 else 1)
            code = jnp.where((lane >= own_n) & (u == base + i), 3 * r + j, code)
    left = 2 * wide
    code = jnp.where((lane >= own_n) & (u >= left) & (u < left + th_len), 3, code)
    code = jnp.where((lane >= own_n) & (u >= left + th_len), 5, code)
    allowed = jnp.zeros((1, own_n + halo_n), jnp.float32)
    for i in range(3):
        for j in range(3):
            flag = pattern_ref[0, 0, 3 * i + j].astype(jnp.float32)
            if (i, j) != (1, 1):
                flag = flag * has(i - 1, j - 1).astype(jnp.float32)
            allowed = jnp.where(code == 3 * i + j, flag, allowed)
    allow[...] = allowed

    for h in range(heads):
        v_s[:, pl.ds((2 * h + 1) * HEAD, HEAD)] = jnp.ones((own_n + halo_n, HEAD), v_s.dtype)

    mod_copy.wait()

    @pl.when(seg == n_seg - 1)
    def _():
        tok_copy.wait()

    own_rows, own_cols = pl.ds(1, th_len), pl.ds(1, tw_len)

    def own_copy(k, target, dst, sem):
        return pltpu.make_async_remote_copy(
            src_ref=outgo.at[k],
            dst_ref=dst,
            send_sem=own_send.at[k],
            recv_sem=sem,
            device_id=(target, a, b),
            device_id_type=MESH,
        )

    def next_copy(k):
        return own_copy(k, jnp.maximum(seg - 1, 0), ext.at[k, :, own_rows, own_cols], own_recv.at[k])

    def fin_copy(k):
        return own_copy(k, lax.rem(k + 1, n_seg), fin, fin_recv)

    def halo_copy(k, d):
        da, db = DIRS[d]
        (r0, rn), (rt, _) = span(da, th_len)
        (c0, cn), (ct, _) = span(db, tw_len)
        return pltpu.make_async_remote_copy(
            src_ref=ext.at[k, :, pl.ds(1 + r0, rn), pl.ds(1 + c0, cn)],
            dst_ref=ext.at[k, :, pl.ds(rt, rn), pl.ds(ct, cn)],
            send_sem=halo_send.at[k, d],
            recv_sem=halo_recv.at[k, d],
            device_id=(seg, a + da, b + db),
            device_id_type=MESH,
        )

    def modulate(base):
        @pl.loop(0, own_n // 16, unroll=UNROLL)
        def _(g):
            start = (base + g * 16) * blocks
            cols = [xs[pl.ds(start + j, 16, stride=blocks), :] for j in range(blocks)]
            total = cols[0]
            for j in range(1, blocks):
                total = total + cols[j]
            mean = jnp.sum(total, axis=-1, keepdims=True) * (1.0 / width)
            cols = [c - mean for c in cols]
            total = cols[0] * cols[0]
            for j in range(1, blocks):
                total = total + cols[j] * cols[j]
            var = jnp.sum(total, axis=-1, keepdims=True) * (1.0 / width)
            scale = lax.rsqrt(var + 1e-06)
            rows = pl.ds(pl.multiple_of(g * 16, 16), 16)
            for j in range(blocks):
                lanes = pl.ds(j * LANE, LANE)
                value = cols[j] * scale * (1.0 + mod[1:2, lanes]) + mod[0:1, lanes]
                xm[rows, lanes] = value.astype(jnp.bfloat16)

    def project(k, first_col, dst, row0, norm):
        if k is not None:

            @pl.when(k == 0)
            def _():
                for i in range(inner // qkv_cols):
                    wq_copy(first_col // qkv_cols + i).wait()

        for i in range(inner // qkv_cols):
            cols = pl.ds(first_col + i * qkv_cols, qkv_cols)
            p = jnp.dot(xm[...], wqkv[:, cols], preferred_element_type=jnp.float32)
            for h in range(qkv_cols // HEAD):
                ph = p[:, h * HEAD : (h + 1) * HEAD]
                if norm:
                    ms = jnp.sum(ph * ph, axis=-1, keepdims=True) * (1.0 / HEAD)
                    ph = ph * lax.rsqrt(ms + 1e-06)
                at = (i * qkv_cols + h * HEAD) * (1 if norm else 2)
                dst[pl.ds(row0, own_n), pl.ds(at, HEAD)] = ph.astype(jnp.bfloat16)

    @pl.loop(0, patches)
    def _(k):
        @pl.when(seg == n_seg - 1)
        def _():
            patch = lax.rem(k + 1, n_seg)

            @pl.loop(0, FP)
            def _(f):
                frame = order_ref[patch * FP + f]
                for c in range(tw_len):
                    x = tok[frame, c].astype(jnp.float32)
                    base = (f * th_len * tw_len + c) * blocks
                    for j in range(blocks):
                        xs[pl.ds(base + j, th_len, stride=tw_len * blocks), :] = x[
                            :, j * LANE : (j + 1) * LANE
                        ]
                for r in range(th_len):
                    base = (f * th_len + r) * tw_len * blocks
                    y = xs[pl.ds(base, tw_len * blocks), :]
                    ext[k, f, 1 + r, 1 : 1 + tw_len] = y.astype(jnp.bfloat16).reshape(
                        tw_len, blocks, LANE
                    )

        @pl.when(seg < n_seg - 1)
        def _():
            next_copy(k).wait_recv()

        for d, (da, db) in enumerate(DIRS):

            @pl.when(has(da, db))
            def _():
                halo_copy(k, d).start()

        @pl.when(seg < n_seg - 1)
        def _():
            @pl.loop(0, FP)
            def _(f):
                for r in range(th_len):
                    y = ext[k, f, 1 + r, 1 : 1 + tw_len]
                    base = (f * th_len + r) * tw_len * blocks
                    xs[pl.ds(base, tw_len * blocks), :] = y.reshape(
                        tw_len * blocks, LANE
                    ).astype(jnp.float32)

        modulate(0)
        project(k, 0, q_s, 0, True)
        project(k, inner, k_s, 0, True)
        project(k, 2 * inner, v_s, 0, False)

        for d, (da, db) in enumerate(DIRS):

            @pl.when(has(-da, -db))
            def _():
                halo_copy(k, d).wait_recv()

        @pl.loop(0, FP)
        def _(f):
            base = (own_n + f * ring_n) * blocks
            for r in (0, th_len + 1):
                y = ext[k, f, r].reshape(wide * blocks, LANE)
                xs[pl.ds(base, wide * blocks), :] = y.astype(jnp.float32)
                base = base + wide * blocks
            for c in (0, tw_len + 1):
                for r in range(th_len):
                    xs[pl.ds(base, blocks), :] = ext[k, f, 1 + r, c].astype(jnp.float32)
                    base = base + blocks

        modulate(own_n)
        project(None, inner, k_s, own_n, True)
        project(None, 2 * inner, v_s, own_n, False)

        allowed = allow[...]
        for h in range(heads):
            lanes = pl.ds(h * HEAD, HEAD)
            s = lax.dot_general(
                q_s[:, lanes],
                k_s[:, lanes],
                (((1,), (1,)), ((), ())),
                preferred_element_type=jnp.float32,
            )
            e = jnp.exp(s * (1.0 / math.sqrt(HEAD))) * allowed
            o = jnp.dot(
                e.astype(jnp.bfloat16),
                v_s[:, pl.ds(2 * h * HEAD, 2 * HEAD)],
                preferred_element_type=jnp.float32,
            )
            att[:, lanes] = (o[:, :HEAD] / o[:, HEAD:]).astype(jnp.bfloat16)

        @pl.when(k == 0)
        def _():
            for i in range(n_out):
                wo_copy(i).wait()

        for i in range(n_out):
            acc = jnp.dot(
                att[...], wout[:, pl.ds(i * out_cols, out_cols)], preferred_element_type=jnp.float32
            )
            for j in range(out_cols // LANE):
                block = i * (out_cols // LANE) + j
                rows = pl.ds(block, own_n, stride=blocks)
                gate = mod[2:3, pl.ds(block * LANE, LANE)]
                xs[rows, :] = xs[rows, :] + gate * acc[:, j * LANE : (j + 1) * LANE]

        @pl.loop(0, FP)
        def _(f):
            for r in range(th_len):
                base = (f * th_len + r) * tw_len * blocks
                y = xs[pl.ds(base, tw_len * blocks), :]
                outgo[k, f, r] = y.astype(jnp.bfloat16).reshape(tw_len, blocks, LANE)

        @pl.when(seg > 0)
        def _():
            next_copy(k).start()

        @pl.when(jnp.logical_and(seg == 0, k < patches - 1))
        def _():
            fin_copy(k).start()

    def emit(read):
        @pl.loop(0, FP)
        def _(f):
            for r in range(th_len):
                y = read(f, r).reshape(tw_len * blocks, LANE).astype(jnp.float32)
                base = (f * th_len + r) * tw_len * blocks
                xs[pl.ds(base, tw_len * blocks), :] = y
            for c in range(tw_len):
                base = (f * th_len * tw_len + c) * blocks
                for j in range(blocks):
                    out_ref[f, c, :, pl.ds(j * LANE, LANE)] = xs[
                        pl.ds(base + j, th_len, stride=tw_len * blocks), :
                    ].astype(jnp.bfloat16)

    @pl.when(seg == 0)
    def _():
        emit(lambda f, r: outgo[patches - 1, f, r])

    @pl.when(seg > 0)
    def _():
        fin_copy(0).wait_recv()
        emit(lambda f, r: fin[f, r])

    @pl.loop(0, patches)
    def _(k):
        @pl.when(jnp.logical_or(seg > 0, k < patches - 1))
        def _():
            next_copy(k).wait_send()

        for d, (da, db) in enumerate(DIRS):

            @pl.when(has(da, db))
            def _():
                halo_copy(k, d).wait_send()


def solution(mesh):
    n_seg, n_th, n_tw = (mesh.shape[name] for name in ("segment", "th", "tw"))

    def on_device(tokens, frame_order, tile_pattern, qkv_weight, out_weight, modulation):
        frames, th_len, tw_len, width = tokens.shape
        inner = out_weight.shape[1]
        blocks = width // LANE
        own_n = FP * th_len * tw_len
        halo_n = FP * (2 * (tw_len + 2) + 2 * th_len)
        all_n = own_n + halo_n
        assert halo_n == own_n and n_seg * FP == frames
        sizes = (n_seg, n_th, n_tw, th_len, tw_len, width, inner)
        bf16, f32 = jnp.bfloat16, jnp.float32
        smem = pl.BlockSpec(memory_space=pltpu.SMEM)
        hbm = pl.BlockSpec(memory_space=pl.ANY)
        dma = pltpu.SemaphoreType.DMA
        out = pl.pallas_call(
            functools.partial(kernel, sizes),
            out_shape=jax.ShapeDtypeStruct((FP, tw_len, th_len, width), bf16),
            in_specs=[smem, smem, hbm, hbm, hbm, hbm],
            out_specs=pl.BlockSpec(memory_space=pltpu.VMEM),
            scratch_shapes=[
                pltpu.VMEM((width, 3 * inner), bf16),
                pltpu.VMEM((inner, width), bf16),
                pltpu.VMEM((3, width), f32),
                pltpu.VMEM((frames, tw_len, th_len, width), bf16),
                pltpu.VMEM((n_seg, FP, th_len + 2, tw_len + 2, blocks, LANE), bf16),
                pltpu.VMEM((n_seg, FP, th_len, tw_len, blocks, LANE), bf16),
                pltpu.VMEM((FP, th_len, tw_len, blocks, LANE), bf16),
                pltpu.VMEM((all_n * blocks, LANE), f32),
                pltpu.VMEM((own_n, width), bf16),
                pltpu.VMEM((own_n, inner), bf16),
                pltpu.VMEM((all_n, inner), bf16),
                pltpu.VMEM((all_n, 2 * inner), bf16),
                pltpu.VMEM((own_n, inner), bf16),
                pltpu.VMEM((1, all_n), f32),
                dma((3 * inner // 512 + width // 512 + 2,)),
                dma((n_seg,)),
                dma((n_seg, 8)),
                dma((n_seg,)),
                dma((n_seg, 8)),
                dma,
            ],
            compiler_params=pltpu.CompilerParams(
                collective_id=0, has_side_effects=True, vmem_limit_bytes=60 * 1024 * 1024
            ),
            name="sections",
        )(
            frame_order,
            tile_pattern,
            tokens.transpose(0, 2, 1, 3),
            qkv_weight,
            out_weight,
            modulation.transpose(1, 0, 2),
        )
        return out.transpose(0, 2, 1, 3)

    in_specs = (
        P(None, "th", "tw", None),
        P(),
        P("th", "tw", None),
        P("segment", None, None),
        P("segment", None, None),
        P("segment", None, None),
    )
    out_specs = P("segment", "th", "tw", None)
    return jax.shard_map(
        on_device, mesh=mesh, in_specs=in_specs, out_specs=out_specs, check_vma=False
    )
```

```python
import functools
import math

import jax
import jax.numpy as jnp
from jax import lax
from jax.experimental import pallas as pl
from jax.experimental.pallas import tpu as pltpu
from jax.sharding import PartitionSpec as P

HEAD = 128
LANE = 128
FP = 4
UNROLL = 3
Q_SCALE = math.log2(math.e) / math.sqrt(HEAD)
MESH = pl.DeviceIdType.MESH
DIRS = [(i, j) for i in (-1, 0, 1) for j in (-1, 0, 1) if (i, j) != (0, 0)]


def span(step, length):
    if step == 0:
        return (0, length), (1, length)
    if step < 0:
        return (0, 1), (length + 1, 1)
    return (length - 1, 1), (0, 1)


def kernel(
    sizes,
    order_ref,
    pattern_ref,
    tokens_hbm,
    wqkv_hbm,
    wout_hbm,
    mod_hbm,
    out_ref,
    wqkv,
    wout,
    mod,
    tok,
    ext,
    outgo,
    fin,
    xs,
    xt,
    xm,
    q_s,
    k_s,
    v_s,
    att,
    allow,
    wsem,
    own_recv,
    halo_recv,
    own_send,
    halo_send,
    fin_recv,
):
    n_seg, n_th, n_tw, th_len, tw_len, width, inner = sizes
    heads = inner // HEAD
    blocks = width // LANE
    own_n = FP * th_len * tw_len
    ring_n = 2 * (tw_len + 2) + 2 * th_len
    halo_n = FP * ring_n
    patches = n_seg
    seg = lax.axis_index("segment")
    a = lax.axis_index("th")
    b = lax.axis_index("tw")

    qkv_cols = 512
    n_qkv = 3 * inner // qkv_cols
    out_cols = 512
    n_out = width // out_cols

    def wq_copy(i):
        cols = pl.ds(i * qkv_cols, qkv_cols)
        return pltpu.make_async_copy(wqkv_hbm.at[0, :, cols], wqkv.at[:, cols], wsem.at[i])

    def wo_copy(i):
        cols = pl.ds(i * out_cols, out_cols)
        return pltpu.make_async_copy(wout_hbm.at[0, :, cols], wout.at[:, cols], wsem.at[n_qkv + i])

    mod_copy = pltpu.make_async_copy(mod_hbm.at[:, 0], mod, wsem.at[n_qkv + n_out])
    tok_copy = pltpu.make_async_copy(tokens_hbm, tok, wsem.at[n_qkv + n_out + 1])
    mod_copy.start()

    @pl.when(seg == n_seg - 1)
    def _():
        tok_copy.start()

    for i in range(n_qkv):
        wq_copy(i).start()
    for i in range(n_out):
        wo_copy(i).start()

    row_cells = (tw_len + 2, blocks, LANE)
    for edge, at in ((a == 0, 0), (a == n_th - 1, th_len + 1)):

        @pl.when(edge)
        def _():
            @pl.loop(0, patches * FP)
            def _(i):
                ext[i // FP, i % FP, at] = jnp.zeros(row_cells, ext.dtype)

    for edge, at in ((b == 0, 0), (b == n_tw - 1, tw_len + 1)):

        @pl.when(edge)
        def _():
            @pl.loop(0, patches * FP)
            def _(i):
                for r in range(th_len + 2):
                    ext[i // FP, i % FP, r, at] = jnp.zeros((blocks, LANE), ext.dtype)

    barrier = pltpu.get_barrier_semaphore()
    for s in range(1, n_seg):
        other = lax.rem(seg + s, n_seg)
        pl.semaphore_signal(barrier, inc=1, device_id=(other, a, b), device_id_type=MESH)

    def has(da, db):
        ok = None
        for pos, step, count in ((a, da, n_th), (b, db, n_tw)):
            if step == 0:
                continue
            here = pos > 0 if step < 0 else pos < count - 1
            ok = here if ok is None else jnp.logical_and(ok, here)
        return ok

    for da, db in DIRS:

        @pl.when(has(da, db))
        def _():
            pl.semaphore_signal(
                barrier, inc=1, device_id=(seg, a + da, b + db), device_id_type=MESH
            )

    near_rows = 1 + (a > 0).astype(jnp.int32) + (a < n_th - 1).astype(jnp.int32)
    near_cols = 1 + (b > 0).astype(jnp.int32) + (b < n_tw - 1).astype(jnp.int32)
    pl.semaphore_wait(barrier, n_seg - 2 + near_rows * near_cols)

    row = lax.broadcasted_iota(jnp.int32, (halo_n, LANE), 0)
    u = row
    for f in range(1, FP):
        u = jnp.where(row >= f * ring_n, row - f * ring_n, u)
    wide = tw_len + 2
    left = 2 * wide
    keep = jnp.zeros((halo_n, LANE), jnp.float32)
    for low, count, i, j in (
        (0, 1, 0, 0),
        (1, tw_len, 0, 1),
        (wide - 1, 1, 0, 2),
        (wide, 1, 2, 0),
        (wide + 1, tw_len, 2, 1),
        (2 * wide - 1, 1, 2, 2),
        (left, th_len, 1, 0),
        (left + th_len, th_len, 1, 2),
    ):
        flag = pattern_ref[0, 0, 3 * i + j].astype(jnp.float32)
        flag = flag * has(i - 1, j - 1).astype(jnp.float32)
        keep = jnp.where((u >= low) & (u < low + count), flag, keep)
    allow[...] = keep
    for h in range(heads):
        lanes = pl.ds((2 * h + 1) * HEAD, HEAD)
        v_s[0:own_n, lanes] = jnp.full(
            (own_n, HEAD), pattern_ref[0, 0, 4].astype(jnp.float32)
        ).astype(v_s.dtype)
        v_s[own_n : own_n + halo_n, lanes] = keep.astype(v_s.dtype)

    mod_copy.wait()
    mod[1:2, :] = 1.0 + mod[1:2, :]

    @pl.when(seg == n_seg - 1)
    def _():
        tok_copy.wait()

    own_rows, own_cols = pl.ds(1, th_len), pl.ds(1, tw_len)

    def own_copy(k, target, dst, sem):
        return pltpu.make_async_remote_copy(
            src_ref=outgo.at[k],
            dst_ref=dst,
            send_sem=own_send.at[k],
            recv_sem=sem,
            device_id=(target, a, b),
            device_id_type=MESH,
        )

    def next_copy(k):
        return own_copy(k, jnp.maximum(seg - 1, 0), ext.at[k, :, own_rows, own_cols], own_recv.at[k])

    def fin_copy(k):
        return own_copy(k, lax.rem(k + 1, n_seg), fin, fin_recv)

    def halo_copy(k, d):
        da, db = DIRS[d]
        (r0, rn), (rt, _) = span(da, th_len)
        (c0, cn), (ct, _) = span(db, tw_len)
        return pltpu.make_async_remote_copy(
            src_ref=ext.at[k, :, pl.ds(1 + r0, rn), pl.ds(1 + c0, cn)],
            dst_ref=ext.at[k, :, pl.ds(rt, rn), pl.ds(ct, cn)],
            send_sem=halo_send.at[k, d],
            recv_sem=halo_recv.at[k, d],
            device_id=(seg, a + da, b + db),
            device_id_type=MESH,
        )

    def modulate(base):
        @pl.loop(0, own_n // 16, unroll=UNROLL)
        def _(g):
            start = (base + g * 16) * blocks
            cols = [xs[pl.ds(start + j, 16, stride=blocks), :] for j in range(blocks)]
            total = cols[0]
            for j in range(1, blocks):
                total = total + cols[j]
            mean = jnp.sum(total, axis=-1, keepdims=True) * (1.0 / width)
            cols = [c - mean for c in cols]
            total = cols[0] * cols[0]
            for j in range(1, blocks):
                total = total + cols[j] * cols[j]
            var = jnp.sum(total, axis=-1, keepdims=True) * (1.0 / width)
            scale = lax.rsqrt(var + 1e-06)
            rows = pl.ds(pl.multiple_of(g * 16, 16), 16)
            for j in range(blocks):
                lanes = pl.ds(j * LANE, LANE)
                value = cols[j] * scale * mod[1:2, lanes] + mod[0:1, lanes]
                xm[rows, lanes] = value.astype(jnp.bfloat16)

    def project(first_col, dst, row0, norm):
        keep = allow[...] if row0 and norm is None else None
        for i in range(inner // qkv_cols):
            cols = pl.ds(first_col + i * qkv_cols, qkv_cols)
            p = jnp.dot(xm[...], wqkv[:, cols], preferred_element_type=jnp.float32)
            for h in range(qkv_cols // HEAD):
                ph = p[:, h * HEAD : (h + 1) * HEAD]
                if norm is not None:
                    ms = jnp.sum(ph * ph, axis=-1, keepdims=True) * (1.0 / HEAD)
                    ph = ph * (lax.rsqrt(ms + 1e-06) * norm)
                elif keep is not None:
                    ph = ph * keep
                at = (i * qkv_cols + h * HEAD) * (2 if norm is None else 1)
                dst[pl.ds(row0, own_n), pl.ds(at, HEAD)] = ph.astype(jnp.bfloat16)

    def bring(k):
        @pl.when(seg == n_seg - 1)
        def _():
            patch = lax.rem(k + 1, n_seg)

            @pl.loop(0, FP)
            def _(f):
                frame = order_ref[patch * FP + f]
                for c in range(tw_len):
                    x = tok[frame, c].astype(jnp.float32)
                    for j in range(blocks):
                        xt[pl.ds(c * blocks + j, th_len, stride=tw_len * blocks), :] = x[
                            :, j * LANE : (j + 1) * LANE
                        ]
                for r in range(th_len):
                    y = xt[pl.ds(r * tw_len * blocks, tw_len * blocks), :]
                    ext[k, f, 1 + r, 1 : 1 + tw_len] = y.astype(jnp.bfloat16).reshape(
                        tw_len, blocks, LANE
                    )

        @pl.when(seg < n_seg - 1)
        def _():
            next_copy(k).wait_recv()

        for d, (da, db) in enumerate(DIRS):

            @pl.when(has(da, db))
            def _():
                halo_copy(k, d).start()

    def project_own(wait):
        for first, dst, norm in ((0, q_s, Q_SCALE), (inner, k_s, 1.0), (2 * inner, v_s, None)):
            if wait:
                for i in range(inner // qkv_cols):
                    wq_copy(first // qkv_cols + i).wait()
            project(first, dst, 0, norm)

    first_seg = seg == n_seg - 1

    @pl.when(jnp.logical_not(first_seg))
    def _():
        for i in range(n_qkv):
            wq_copy(i).wait()
        for i in range(n_out):
            wo_copy(i).wait()

    bring(0)

    @pl.loop(0, patches)
    def _(k):
        @pl.loop(0, FP)
        def _(f):
            for r in range(th_len):
                y = ext[k, f, 1 + r, 1 : 1 + tw_len]
                base = (f * th_len + r) * tw_len * blocks
                xs[pl.ds(base, tw_len * blocks), :] = y.reshape(tw_len * blocks, LANE).astype(
                    jnp.float32
                )

        fresh = jnp.logical_and(first_seg, k == 0)
        modulate(0)

        @pl.when(fresh)
        def _():
            project_own(True)

        @pl.when(jnp.logical_not(fresh))
        def _():
            project_own(False)

        for d, (da, db) in enumerate(DIRS):

            @pl.when(has(-da, -db))
            def _():
                halo_copy(k, d).wait_recv()

        @pl.loop(0, FP)
        def _(f):
            base = (own_n + f * ring_n) * blocks
            for r in (0, th_len + 1):
                y = ext[k, f, r].reshape(wide * blocks, LANE)
                xs[pl.ds(base, wide * blocks), :] = y.astype(jnp.float32)
                base = base + wide * blocks
            for c in (0, tw_len + 1):
                for r in range(th_len):
                    xs[pl.ds(base, blocks), :] = ext[k, f, 1 + r, c].astype(jnp.float32)
                    base = base + blocks

        modulate(own_n)
        project(inner, k_s, own_n, 1.0)
        project(2 * inner, v_s, own_n, None)

        @pl.when(k < patches - 1)
        def _():
            bring(k + 1)

        for h in range(heads):
            lanes = pl.ds(h * HEAD, HEAD)
            s = lax.dot_general(
                q_s[:, lanes],
                k_s[:, lanes],
                (((1,), (1,)), ((), ())),
                preferred_element_type=jnp.float32,
            )
            e = jnp.exp2(s)
            o = jnp.dot(
                e.astype(jnp.bfloat16),
                v_s[:, pl.ds(2 * h * HEAD, 2 * HEAD)],
                preferred_element_type=jnp.float32,
            )
            att[:, lanes] = (o[:, :HEAD] / o[:, HEAD:]).astype(jnp.bfloat16)

        @pl.when(fresh)
        def _():
            for i in range(n_out):
                wo_copy(i).wait()

        for i in range(n_out):
            acc = jnp.dot(
                att[...], wout[:, pl.ds(i * out_cols, out_cols)], preferred_element_type=jnp.float32
            )
            for j in range(out_cols // LANE):
                block = i * (out_cols // LANE) + j
                rows = pl.ds(block, own_n, stride=blocks)
                gate = mod[2:3, pl.ds(block * LANE, LANE)]
                xs[rows, :] = xs[rows, :] + gate * acc[:, j * LANE : (j + 1) * LANE]

        @pl.loop(0, FP)
        def _(f):
            for r in range(th_len):
                base = (f * th_len + r) * tw_len * blocks
                y = xs[pl.ds(base, tw_len * blocks), :]
                outgo[k, f, r] = y.astype(jnp.bfloat16).reshape(tw_len, blocks, LANE)

        @pl.when(seg > 0)
        def _():
            next_copy(k).start()

        @pl.when(jnp.logical_and(seg == 0, k < patches - 1))
        def _():
            fin_copy(k).start()

    def emit(read):
        @pl.loop(0, FP)
        def _(f):
            for r in range(th_len):
                y = read(f, r).reshape(tw_len * blocks, LANE).astype(jnp.float32)
                base = (f * th_len + r) * tw_len * blocks
                xs[pl.ds(base, tw_len * blocks), :] = y
            for c in range(tw_len):
                base = (f * th_len * tw_len + c) * blocks
                for j in range(blocks):
                    out_ref[f, c, :, pl.ds(j * LANE, LANE)] = xs[
                        pl.ds(base + j, th_len, stride=tw_len * blocks), :
                    ].astype(jnp.bfloat16)

    @pl.when(seg == 0)
    def _():
        emit(lambda f, r: outgo[patches - 1, f, r])

    @pl.when(seg > 0)
    def _():
        fin_copy(0).wait_recv()
        emit(lambda f, r: fin[f, r])

    @pl.loop(0, patches)
    def _(k):
        @pl.when(jnp.logical_or(seg > 0, k < patches - 1))
        def _():
            next_copy(k).wait_send()

        for d, (da, db) in enumerate(DIRS):

            @pl.when(has(da, db))
            def _():
                halo_copy(k, d).wait_send()


def solution(mesh):
    n_seg, n_th, n_tw = (mesh.shape[name] for name in ("segment", "th", "tw"))

    def on_device(tokens, frame_order, tile_pattern, qkv_weight, out_weight, modulation):
        frames, th_len, tw_len, width = tokens.shape
        inner = out_weight.shape[1]
        blocks = width // LANE
        own_n = FP * th_len * tw_len
        halo_n = FP * (2 * (tw_len + 2) + 2 * th_len)
        all_n = own_n + halo_n
        assert halo_n == own_n and n_seg * FP == frames
        sizes = (n_seg, n_th, n_tw, th_len, tw_len, width, inner)
        bf16, f32 = jnp.bfloat16, jnp.float32
        smem = pl.BlockSpec(memory_space=pltpu.SMEM)
        hbm = pl.BlockSpec(memory_space=pl.ANY)
        dma = pltpu.SemaphoreType.DMA
        out = pl.pallas_call(
            functools.partial(kernel, sizes),
            out_shape=jax.ShapeDtypeStruct((FP, tw_len, th_len, width), bf16),
            in_specs=[smem, smem, hbm, hbm, hbm, hbm],
            out_specs=pl.BlockSpec(memory_space=pltpu.VMEM),
            scratch_shapes=[
                pltpu.VMEM((width, 3 * inner), bf16),
                pltpu.VMEM((inner, width), bf16),
                pltpu.VMEM((3, width), f32),
                pltpu.VMEM((frames, tw_len, th_len, width), bf16),
                pltpu.VMEM((n_seg, FP, th_len + 2, tw_len + 2, blocks, LANE), bf16),
                pltpu.VMEM((n_seg, FP, th_len, tw_len, blocks, LANE), bf16),
                pltpu.VMEM((FP, th_len, tw_len, blocks, LANE), bf16),
                pltpu.VMEM((all_n * blocks, LANE), f32),
                pltpu.VMEM((th_len * tw_len * blocks, LANE), f32),
                pltpu.VMEM((own_n, width), bf16),
                pltpu.VMEM((own_n, inner), bf16),
                pltpu.VMEM((all_n, inner), bf16),
                pltpu.VMEM((all_n, 2 * inner), bf16),
                pltpu.VMEM((own_n, inner), bf16),
                pltpu.VMEM((halo_n, LANE), f32),
                dma((3 * inner // 512 + width // 512 + 2,)),
                dma((n_seg,)),
                dma((n_seg, 8)),
                dma((n_seg,)),
                dma((n_seg, 8)),
                dma,
            ],
            compiler_params=pltpu.CompilerParams(
                collective_id=0, has_side_effects=True, vmem_limit_bytes=60 * 1024 * 1024
            ),
            name="sections",
        )(
            frame_order,
            tile_pattern,
            tokens.transpose(0, 2, 1, 3),
            qkv_weight,
            out_weight,
            modulation.transpose(1, 0, 2),
        )
        return out.transpose(0, 2, 1, 3)

    in_specs = (
        P(None, "th", "tw", None),
        P(),
        P("th", "tw", None),
        P("segment", None, None),
        P("segment", None, None),
        P("segment", None, None),
    )
    out_specs = P("segment", "th", "tw", None)
    return jax.shard_map(
        on_device, mesh=mesh, in_specs=in_specs, out_specs=out_specs, check_vma=False
    )
```

```python
import functools
import math

import jax
import jax.numpy as jnp
from jax import lax
from jax.experimental import pallas as pl
from jax.experimental.pallas import tpu as pltpu
from jax.sharding import PartitionSpec as P

HEAD = 128
LANE = 128
FP = 4
UNROLL = 6
PIECES = 2
Q_SCALE = math.log2(math.e) / math.sqrt(HEAD)
MESH = pl.DeviceIdType.MESH
DIRS = [(i, j) for i in (-1, 0, 1) for j in (-1, 0, 1) if (i, j) != (0, 0)]


def key_split(count):
    return -(-count // LANE) * LANE


def span(step, length):
    if step == 0:
        return (0, length), (1, length)
    if step < 0:
        return (0, 1), (length + 1, 1)
    return (length - 1, 1), (0, 1)


def kernel(
    sizes,
    order_ref,
    pattern_ref,
    tokens_hbm,
    wqkv_hbm,
    wout_hbm,
    mod_hbm,
    out_ref,
    wqkv,
    wout,
    mod,
    tok,
    ext,
    outgo,
    fin,
    xs,
    xt,
    xm,
    q_s,
    k_s,
    v_s,
    att,
    allow,
    wsem,
    own_recv,
    halo_recv,
    own_send,
    halo_send,
    fin_recv,
):
    n_seg, n_th, n_tw, th_len, tw_len, width, inner = sizes
    heads = inner // HEAD
    blocks = width // LANE
    own_n = FP * th_len * tw_len
    ring_n = 2 * (tw_len + 2) + 2 * th_len
    halo_n = FP * ring_n
    patches = n_seg
    split = key_split(own_n)
    seg = lax.axis_index("segment")
    a = lax.axis_index("th")
    b = lax.axis_index("tw")

    qkv_cols = 512
    n_qkv = 3 * inner // qkv_cols
    out_cols = 512
    n_out = width // out_cols

    def wq_copy(i):
        cols = pl.ds(i * qkv_cols, qkv_cols)
        return pltpu.make_async_copy(wqkv_hbm.at[0, :, cols], wqkv.at[:, cols], wsem.at[i])

    def wo_copy(i):
        cols = pl.ds(i * out_cols, out_cols)
        return pltpu.make_async_copy(wout_hbm.at[0, :, cols], wout.at[:, cols], wsem.at[n_qkv + i])

    mod_copy = pltpu.make_async_copy(mod_hbm.at[:, 0], mod, wsem.at[n_qkv + n_out])
    tok_copy = pltpu.make_async_copy(tokens_hbm, tok, wsem.at[n_qkv + n_out + 1])
    mod_copy.start()

    @pl.when(seg == n_seg - 1)
    def _():
        tok_copy.start()

    for i in range(n_qkv):
        wq_copy(i).start()
    for i in range(n_out):
        wo_copy(i).start()

    row_cells = (tw_len + 2, blocks, LANE)
    for edge, at in ((a == 0, 0), (a == n_th - 1, th_len + 1)):

        @pl.when(edge)
        def _():
            @pl.loop(0, patches * FP)
            def _(i):
                ext[i // FP, i % FP, at] = jnp.zeros(row_cells, ext.dtype)

    for edge, at in ((b == 0, 0), (b == n_tw - 1, tw_len + 1)):

        @pl.when(edge)
        def _():
            @pl.loop(0, patches * FP)
            def _(i):
                for r in range(th_len + 2):
                    ext[i // FP, i % FP, r, at] = jnp.zeros((blocks, LANE), ext.dtype)

    barrier = pltpu.get_barrier_semaphore()
    for s in range(1, n_seg):
        other = lax.rem(seg + s, n_seg)
        pl.semaphore_signal(barrier, inc=1, device_id=(other, a, b), device_id_type=MESH)

    def has(da, db):
        ok = None
        for pos, step, count in ((a, da, n_th), (b, db, n_tw)):
            if step == 0:
                continue
            here = pos > 0 if step < 0 else pos < count - 1
            ok = here if ok is None else jnp.logical_and(ok, here)
        return ok

    for da, db in DIRS:

        @pl.when(has(da, db))
        def _():
            pl.semaphore_signal(
                barrier, inc=1, device_id=(seg, a + da, b + db), device_id_type=MESH
            )

    near_rows = 1 + (a > 0).astype(jnp.int32) + (a < n_th - 1).astype(jnp.int32)
    near_cols = 1 + (b > 0).astype(jnp.int32) + (b < n_tw - 1).astype(jnp.int32)
    pl.semaphore_wait(barrier, n_seg - 2 + near_rows * near_cols)

    row = lax.broadcasted_iota(jnp.int32, (halo_n, LANE), 0)
    u = row
    for f in range(1, FP):
        u = jnp.where(row >= f * ring_n, row - f * ring_n, u)
    wide = tw_len + 2
    left = 2 * wide
    keep = jnp.zeros((halo_n, LANE), jnp.float32)
    for low, count, i, j in (
        (0, 1, 0, 0),
        (1, tw_len, 0, 1),
        (wide - 1, 1, 0, 2),
        (wide, 1, 2, 0),
        (wide + 1, tw_len, 2, 1),
        (2 * wide - 1, 1, 2, 2),
        (left, th_len, 1, 0),
        (left + th_len, th_len, 1, 2),
    ):
        flag = pattern_ref[0, 0, 3 * i + j].astype(jnp.float32)
        flag = flag * has(i - 1, j - 1).astype(jnp.float32)
        keep = jnp.where((u >= low) & (u < low + count), flag, keep)
    allow[...] = keep
    for h in range(heads):
        lanes = pl.ds((2 * h + 1) * HEAD, HEAD)
        v_s[0:own_n, lanes] = jnp.full(
            (own_n, HEAD), pattern_ref[0, 0, 4].astype(jnp.float32)
        ).astype(v_s.dtype)
        v_s[split : split + halo_n, lanes] = keep.astype(v_s.dtype)
    gap = split - own_n
    for start in (own_n, split + halo_n):
        for i in range(0, 2 * inner, 512):
            v_s[start : start + gap, i : i + 512] = jnp.zeros((gap, 512), v_s.dtype)

    @pl.loop(0, heads)
    def _(h):
        k_s[pl.ds(pl.multiple_of(h * HEAD, HEAD), HEAD), :] = jnp.zeros(
            (HEAD, 2 * split), k_s.dtype
        )

    mod_copy.wait()
    mod[1:2, :] = 1.0 + mod[1:2, :]

    @pl.when(seg == n_seg - 1)
    def _():
        tok_copy.wait()

    own_rows, own_cols = pl.ds(1, th_len), pl.ds(1, tw_len)

    piece_n = FP // PIECES

    def own_copy(k, p, target, dst, sem):
        return pltpu.make_async_remote_copy(
            src_ref=outgo.at[k, pl.ds(p * piece_n, piece_n)],
            dst_ref=dst,
            send_sem=own_send.at[k, p],
            recv_sem=sem,
            device_id=(target, a, b),
            device_id_type=MESH,
        )

    def next_copy(k, p):
        dst = ext.at[k, pl.ds(p * piece_n, piece_n), own_rows, own_cols]
        return own_copy(k, p, jnp.maximum(seg - 1, 0), dst, own_recv.at[k, p])

    def fin_copy(k, p):
        dst = fin.at[pl.ds(p * piece_n, piece_n)]
        return own_copy(k, p, lax.rem(k + 1, n_seg), dst, fin_recv.at[p])

    def halo_copy(k, p, d):
        da, db = DIRS[d]
        (r0, rn), (rt, _) = span(da, th_len)
        (c0, cn), (ct, _) = span(db, tw_len)
        frames = pl.ds(p * piece_n, piece_n)
        return pltpu.make_async_remote_copy(
            src_ref=ext.at[k, frames, pl.ds(1 + r0, rn), pl.ds(1 + c0, cn)],
            dst_ref=ext.at[k, frames, pl.ds(rt, rn), pl.ds(ct, cn)],
            send_sem=halo_send.at[k, p, d],
            recv_sem=halo_recv.at[k, p, d],
            device_id=(seg, a + da, b + db),
            device_id_type=MESH,
        )

    def modulate(base):
        @pl.loop(0, own_n // 16, unroll=UNROLL)
        def _(g):
            start = (base + g * 16) * blocks
            cols = [xs[pl.ds(start + j, 16, stride=blocks), :] for j in range(blocks)]
            total = cols[0]
            for j in range(1, blocks):
                total = total + cols[j]
            mean = jnp.sum(total, axis=-1, keepdims=True) * (1.0 / width)
            cols = [c - mean for c in cols]
            total = cols[0] * cols[0]
            for j in range(1, blocks):
                total = total + cols[j] * cols[j]
            var = jnp.sum(total, axis=-1, keepdims=True) * (1.0 / width)
            scale = lax.rsqrt(var + 1e-06)
            rows = pl.ds(pl.multiple_of(g * 16, 16), 16)
            for j in range(blocks):
                lanes = pl.ds(j * LANE, LANE)
                value = cols[j] * scale * mod[1:2, lanes] + mod[0:1, lanes]
                xm[rows, lanes] = value.astype(jnp.bfloat16)

    def project(first_col, dst, row0, norm):
        keep = allow[...] if row0 and norm is None else None
        for i in range(inner // qkv_cols):
            cols = pl.ds(first_col + i * qkv_cols, qkv_cols)
            p = jnp.dot(xm[...], wqkv[:, cols], preferred_element_type=jnp.float32)
            for h in range(qkv_cols // HEAD):
                ph = p[:, h * HEAD : (h + 1) * HEAD]
                if norm is not None:
                    ms = jnp.sum(ph * ph, axis=-1, keepdims=True) * (1.0 / HEAD)
                    ph = ph * (lax.rsqrt(ms + 1e-06) * norm)
                elif keep is not None:
                    ph = ph * keep
                at = (i * qkv_cols + h * HEAD) * (2 if norm is None else 1)
                if norm == 1.0:
                    dst[pl.ds(at, HEAD), pl.ds(row0, own_n)] = ph.T.astype(jnp.bfloat16)
                else:
                    dst[pl.ds(row0, own_n), pl.ds(at, HEAD)] = ph.astype(jnp.bfloat16)

    def bring(k, p):
        @pl.when(seg == n_seg - 1)
        def _():
            patch = lax.rem(k + 1, n_seg)

            @pl.loop(p * piece_n, (p + 1) * piece_n)
            def _(f):
                frame = order_ref[patch * FP + f]
                for c in range(tw_len):
                    x = tok[frame, c].astype(jnp.float32)
                    for j in range(blocks):
                        xt[pl.ds(c * blocks + j, th_len, stride=tw_len * blocks), :] = x[
                            :, j * LANE : (j + 1) * LANE
                        ]
                for r in range(th_len):
                    y = xt[pl.ds(r * tw_len * blocks, tw_len * blocks), :]
                    ext[k, f, 1 + r, 1 : 1 + tw_len] = y.astype(jnp.bfloat16).reshape(
                        tw_len, blocks, LANE
                    )

        @pl.when(seg < n_seg - 1)
        def _():
            next_copy(k, p).wait_recv()

        for d, (da, db) in enumerate(DIRS):

            @pl.when(has(da, db))
            def _():
                halo_copy(k, p, d).start()

    def project_own(wait):
        for first, dst, norm in ((0, q_s, Q_SCALE), (inner, k_s, 1.0), (2 * inner, v_s, None)):
            if wait:
                for i in range(inner // qkv_cols):
                    wq_copy(first // qkv_cols + i).wait()
            project(first, dst, 0, norm)

    first_seg = seg == n_seg - 1

    @pl.when(jnp.logical_not(first_seg))
    def _():
        for i in range(n_qkv):
            wq_copy(i).wait()
        for i in range(n_out):
            wo_copy(i).wait()

    for p in range(PIECES):
        bring(0, p)

    @pl.loop(0, patches)
    def _(k):
        @pl.loop(0, FP)
        def _(f):
            for r in range(th_len):
                y = ext[k, f, 1 + r, 1 : 1 + tw_len]
                base = (f * th_len + r) * tw_len * blocks
                xs[pl.ds(base, tw_len * blocks), :] = y.reshape(tw_len * blocks, LANE).astype(
                    jnp.float32
                )

        fresh = jnp.logical_and(first_seg, k == 0)
        modulate(0)

        @pl.when(fresh)
        def _():
            project_own(True)

        @pl.when(jnp.logical_not(fresh))
        def _():
            project_own(False)

        for d, (da, db) in enumerate(DIRS):

            @pl.when(has(-da, -db))
            def _():
                for p in range(PIECES):
                    halo_copy(k, p, d).wait_recv()

        @pl.loop(0, FP)
        def _(f):
            base = (own_n + f * ring_n) * blocks
            for r in (0, th_len + 1):
                y = ext[k, f, r].reshape(wide * blocks, LANE)
                xs[pl.ds(base, wide * blocks), :] = y.astype(jnp.float32)
                base = base + wide * blocks
            for c in (0, tw_len + 1):
                for r in range(th_len):
                    xs[pl.ds(base, blocks), :] = ext[k, f, 1 + r, c].astype(jnp.float32)
                    base = base + blocks

        modulate(own_n)
        project(inner, k_s, split, 1.0)
        project(2 * inner, v_s, split, None)

        @pl.when(k < patches - 1)
        def _():
            for p in range(PIECES):
                bring(k + 1, p)

        for h in range(heads):
            lanes = pl.ds(h * HEAD, HEAD)
            s = lax.dot_general(
                q_s[:, lanes],
                k_s[lanes, :],
                (((1,), (0,)), ((), ())),
                preferred_element_type=jnp.float32,
            )
            e = jnp.exp2(s)
            o = jnp.dot(
                e.astype(jnp.bfloat16),
                v_s[:, pl.ds(2 * h * HEAD, 2 * HEAD)],
                preferred_element_type=jnp.float32,
            )
            att[:, lanes] = (o[:, :HEAD] / o[:, HEAD:]).astype(jnp.bfloat16)

        @pl.when(fresh)
        def _():
            for i in range(n_out):
                wo_copy(i).wait()

        for i in range(n_out):
            acc = jnp.dot(
                att[...], wout[:, pl.ds(i * out_cols, out_cols)], preferred_element_type=jnp.float32
            )
            for j in range(out_cols // LANE):
                block = i * (out_cols // LANE) + j
                rows = pl.ds(block, own_n, stride=blocks)
                gate = mod[2:3, pl.ds(block * LANE, LANE)]
                xs[rows, :] = xs[rows, :] + gate * acc[:, j * LANE : (j + 1) * LANE]

        for p in range(PIECES):

            @pl.loop(p * piece_n, (p + 1) * piece_n)
            def _(f):
                for r in range(th_len):
                    base = (f * th_len + r) * tw_len * blocks
                    y = xs[pl.ds(base, tw_len * blocks), :]
                    outgo[k, f, r] = y.astype(jnp.bfloat16).reshape(tw_len, blocks, LANE)

            @pl.when(seg > 0)
            def _():
                next_copy(k, p).start()

            @pl.when(jnp.logical_and(seg == 0, k < patches - 1))
            def _():
                fin_copy(k, p).start()

    def emit(read):
        @pl.loop(0, FP)
        def _(f):
            for r in range(th_len):
                y = read(f, r).reshape(tw_len * blocks, LANE).astype(jnp.float32)
                base = (f * th_len + r) * tw_len * blocks
                xs[pl.ds(base, tw_len * blocks), :] = y
            for c in range(tw_len):
                base = (f * th_len * tw_len + c) * blocks
                for j in range(blocks):
                    out_ref[f, c, :, pl.ds(j * LANE, LANE)] = xs[
                        pl.ds(base + j, th_len, stride=tw_len * blocks), :
                    ].astype(jnp.bfloat16)

    @pl.when(seg == 0)
    def _():
        emit(lambda f, r: outgo[patches - 1, f, r])

    @pl.when(seg > 0)
    def _():
        for p in range(PIECES):
            fin_copy(0, p).wait_recv()
        emit(lambda f, r: fin[f, r])

    @pl.loop(0, patches)
    def _(k):
        @pl.when(jnp.logical_or(seg > 0, k < patches - 1))
        def _():
            for p in range(PIECES):
                next_copy(k, p).wait_send()

        for d, (da, db) in enumerate(DIRS):

            @pl.when(has(da, db))
            def _():
                for p in range(PIECES):
                    halo_copy(k, p, d).wait_send()


def solution(mesh):
    n_seg, n_th, n_tw = (mesh.shape[name] for name in ("segment", "th", "tw"))

    def on_device(tokens, frame_order, tile_pattern, qkv_weight, out_weight, modulation):
        frames, th_len, tw_len, width = tokens.shape
        inner = out_weight.shape[1]
        blocks = width // LANE
        own_n = FP * th_len * tw_len
        halo_n = FP * (2 * (tw_len + 2) + 2 * th_len)
        all_n = own_n + halo_n
        assert halo_n == own_n and n_seg * FP == frames
        sizes = (n_seg, n_th, n_tw, th_len, tw_len, width, inner)
        bf16, f32 = jnp.bfloat16, jnp.float32
        smem = pl.BlockSpec(memory_space=pltpu.SMEM)
        hbm = pl.BlockSpec(memory_space=pl.ANY)
        dma = pltpu.SemaphoreType.DMA
        out = pl.pallas_call(
            functools.partial(kernel, sizes),
            out_shape=jax.ShapeDtypeStruct((FP, tw_len, th_len, width), bf16),
            in_specs=[smem, smem, hbm, hbm, hbm, hbm],
            out_specs=pl.BlockSpec(memory_space=pltpu.VMEM),
            scratch_shapes=[
                pltpu.VMEM((width, 3 * inner), bf16),
                pltpu.VMEM((inner, width), bf16),
                pltpu.VMEM((3, width), f32),
                pltpu.VMEM((frames, tw_len, th_len, width), bf16),
                pltpu.VMEM((n_seg, FP, th_len + 2, tw_len + 2, blocks, LANE), bf16),
                pltpu.VMEM((n_seg, FP, th_len, tw_len, blocks, LANE), bf16),
                pltpu.VMEM((FP, th_len, tw_len, blocks, LANE), bf16),
                pltpu.VMEM((all_n * blocks, LANE), f32),
                pltpu.VMEM((th_len * tw_len * blocks, LANE), f32),
                pltpu.VMEM((own_n, width), bf16),
                pltpu.VMEM((own_n, inner), bf16),
                pltpu.VMEM((inner, 2 * key_split(own_n)), bf16),
                pltpu.VMEM((2 * key_split(own_n), 2 * inner), bf16),
                pltpu.VMEM((own_n, inner), bf16),
                pltpu.VMEM((halo_n, LANE), f32),
                dma((3 * inner // 512 + width // 512 + 2,)),
                dma((n_seg, PIECES)),
                dma((n_seg, PIECES, 8)),
                dma((n_seg, PIECES)),
                dma((n_seg, PIECES, 8)),
                dma((PIECES,)),
            ],
            compiler_params=pltpu.CompilerParams(
                collective_id=0, has_side_effects=True, vmem_limit_bytes=60 * 1024 * 1024
            ),
            name="sections",
        )(
            frame_order,
            tile_pattern,
            tokens.transpose(0, 2, 1, 3),
            qkv_weight,
            out_weight,
            modulation.transpose(1, 0, 2),
        )
        return out.transpose(0, 2, 1, 3)

    in_specs = (
        P(None, "th", "tw", None),
        P(),
        P("th", "tw", None),
        P("segment", None, None),
        P("segment", None, None),
        P("segment", None, None),
    )
    out_specs = P("segment", "th", "tw", None)
    return jax.shard_map(
        on_device, mesh=mesh, in_specs=in_specs, out_specs=out_specs, check_vma=False
    )
```

```python
import functools
import math

import jax
import jax.numpy as jnp
from jax import lax
from jax.experimental import pallas as pl
from jax.experimental.pallas import tpu as pltpu
from jax.sharding import PartitionSpec as P

HEAD = 128
LANE = 128
FP = 4
UNROLL = 6
PIECES = 2
Q_SCALE = math.log2(math.e) / math.sqrt(HEAD)
MESH = pl.DeviceIdType.MESH
DIRS = [(i, j) for i in (-1, 0, 1) for j in (-1, 0, 1) if (i, j) != (0, 0)]


def key_split(count):
    return -(-count // LANE) * LANE


def span(step, length):
    if step == 0:
        return (0, length), (1, length)
    if step < 0:
        return (0, 1), (length + 1, 1)
    return (length - 1, 1), (0, 1)


def kernel(
    sizes,
    order_ref,
    pattern_ref,
    tokens_hbm,
    wqkv_hbm,
    wout_hbm,
    mod_hbm,
    out_ref,
    wqkv,
    wout,
    mod,
    tok,
    ext,
    outgo,
    fin,
    xs,
    xt,
    xm,
    q_s,
    k_s,
    v_s,
    att,
    allow,
    wsem,
    own_recv,
    halo_recv,
    own_send,
    halo_send,
    fin_recv,
):
    n_seg, n_th, n_tw, th_len, tw_len, width, inner = sizes
    heads = inner // HEAD
    blocks = width // LANE
    own_n = FP * th_len * tw_len
    ring_n = 2 * (tw_len + 2) + 2 * th_len
    halo_n = FP * ring_n
    patches = n_seg
    split = key_split(own_n)
    seg = lax.axis_index("segment")
    a = lax.axis_index("th")
    b = lax.axis_index("tw")

    qkv_cols = 512
    n_qkv = 3 * inner // qkv_cols
    out_cols = 512
    n_out = width // out_cols

    def wq_copy(i):
        cols = pl.ds(i * qkv_cols, qkv_cols)
        return pltpu.make_async_copy(wqkv_hbm.at[0, :, cols], wqkv.at[:, cols], wsem.at[i])

    def wo_copy(i):
        cols = pl.ds(i * out_cols, out_cols)
        return pltpu.make_async_copy(wout_hbm.at[0, :, cols], wout.at[:, cols], wsem.at[n_qkv + i])

    mod_copy = pltpu.make_async_copy(mod_hbm.at[:, 0], mod, wsem.at[n_qkv + n_out])
    tok_copy = pltpu.make_async_copy(tokens_hbm, tok, wsem.at[n_qkv + n_out + 1])
    mod_copy.start()

    @pl.when(seg == n_seg - 1)
    def _():
        tok_copy.start()

    for i in range(n_qkv):
        wq_copy(i).start()
    for i in range(n_out):
        wo_copy(i).start()

    row_cells = (tw_len + 2, blocks, LANE)
    for edge, at in ((a == 0, 0), (a == n_th - 1, th_len + 1)):

        @pl.when(edge)
        def _():
            @pl.loop(0, patches * FP)
            def _(i):
                ext[i // FP, i % FP, at] = jnp.zeros(row_cells, ext.dtype)

    for edge, at in ((b == 0, 0), (b == n_tw - 1, tw_len + 1)):

        @pl.when(edge)
        def _():
            @pl.loop(0, patches * FP)
            def _(i):
                for r in range(th_len + 2):
                    ext[i // FP, i % FP, r, at] = jnp.zeros((blocks, LANE), ext.dtype)

    barrier = pltpu.get_barrier_semaphore()
    for s in range(1, n_seg):
        other = lax.rem(seg + s, n_seg)
        pl.semaphore_signal(barrier, inc=1, device_id=(other, a, b), device_id_type=MESH)

    def has(da, db):
        ok = None
        for pos, step, count in ((a, da, n_th), (b, db, n_tw)):
            if step == 0:
                continue
            here = pos > 0 if step < 0 else pos < count - 1
            ok = here if ok is None else jnp.logical_and(ok, here)
        return ok

    for da, db in DIRS:

        @pl.when(has(da, db))
        def _():
            pl.semaphore_signal(
                barrier, inc=1, device_id=(seg, a + da, b + db), device_id_type=MESH
            )

    row = lax.broadcasted_iota(jnp.int32, (halo_n, LANE), 0)
    u = row
    for f in range(1, FP):
        u = jnp.where(row >= f * ring_n, row - f * ring_n, u)
    wide = tw_len + 2
    left = 2 * wide
    keep = jnp.zeros((halo_n, LANE), jnp.float32)
    for low, count, i, j in (
        (0, 1, 0, 0),
        (1, tw_len, 0, 1),
        (wide - 1, 1, 0, 2),
        (wide, 1, 2, 0),
        (wide + 1, tw_len, 2, 1),
        (2 * wide - 1, 1, 2, 2),
        (left, th_len, 1, 0),
        (left + th_len, th_len, 1, 2),
    ):
        flag = pattern_ref[0, 0, 3 * i + j].astype(jnp.float32)
        flag = flag * has(i - 1, j - 1).astype(jnp.float32)
        keep = jnp.where((u >= low) & (u < low + count), flag, keep)
    allow[...] = keep
    for h in range(heads):
        lanes = pl.ds((2 * h + 1) * HEAD, HEAD)
        v_s[0:own_n, lanes] = jnp.full(
            (own_n, HEAD), pattern_ref[0, 0, 4].astype(jnp.float32)
        ).astype(v_s.dtype)
        v_s[split : split + halo_n, lanes] = keep.astype(v_s.dtype)
    gap = split - own_n
    for start in (own_n, split + halo_n):
        for i in range(0, 2 * inner, 512):
            v_s[start : start + gap, i : i + 512] = jnp.zeros((gap, 512), v_s.dtype)

    @pl.loop(0, heads)
    def _(h):
        k_s[pl.ds(pl.multiple_of(h * HEAD, HEAD), HEAD), :] = jnp.zeros(
            (HEAD, 2 * split), k_s.dtype
        )

    near_rows = 1 + (a > 0).astype(jnp.int32) + (a < n_th - 1).astype(jnp.int32)
    near_cols = 1 + (b > 0).astype(jnp.int32) + (b < n_tw - 1).astype(jnp.int32)
    pl.semaphore_wait(barrier, n_seg - 2 + near_rows * near_cols)

    mod_copy.wait()
    mod[1:2, :] = 1.0 + mod[1:2, :]

    @pl.when(seg == n_seg - 1)
    def _():
        tok_copy.wait()

    own_rows, own_cols = pl.ds(1, th_len), pl.ds(1, tw_len)

    piece_n = FP // PIECES

    def own_copy(k, p, target, dst, sem):
        return pltpu.make_async_remote_copy(
            src_ref=outgo.at[k, pl.ds(p * piece_n, piece_n)],
            dst_ref=dst,
            send_sem=own_send.at[k, p],
            recv_sem=sem,
            device_id=(target, a, b),
            device_id_type=MESH,
        )

    def next_copy(k, p):
        dst = ext.at[k, pl.ds(p * piece_n, piece_n), own_rows, own_cols]
        return own_copy(k, p, jnp.maximum(seg - 1, 0), dst, own_recv.at[k, p])

    def fin_copy(k, p):
        dst = fin.at[pl.ds(p * piece_n, piece_n)]
        return own_copy(k, p, lax.rem(k + 1, n_seg), dst, fin_recv.at[p])

    def halo_copy(k, p, d):
        da, db = DIRS[d]
        (r0, rn), (rt, _) = span(da, th_len)
        (c0, cn), (ct, _) = span(db, tw_len)
        frames = pl.ds(p * piece_n, piece_n)
        return pltpu.make_async_remote_copy(
            src_ref=ext.at[k, frames, pl.ds(1 + r0, rn), pl.ds(1 + c0, cn)],
            dst_ref=ext.at[k, frames, pl.ds(rt, rn), pl.ds(ct, cn)],
            send_sem=halo_send.at[k, p, d],
            recv_sem=halo_recv.at[k, p, d],
            device_id=(seg, a + da, b + db),
            device_id_type=MESH,
        )

    def modulate(base):
        @pl.loop(0, own_n // 16, unroll=UNROLL)
        def _(g):
            start = (base + g * 16) * blocks
            cols = [xs[pl.ds(start + j, 16, stride=blocks), :] for j in range(blocks)]
            total = cols[0]
            for j in range(1, blocks):
                total = total + cols[j]
            mean = jnp.sum(total, axis=-1, keepdims=True) * (1.0 / width)
            cols = [c - mean for c in cols]
            total = cols[0] * cols[0]
            for j in range(1, blocks):
                total = total + cols[j] * cols[j]
            var = jnp.sum(total, axis=-1, keepdims=True) * (1.0 / width)
            scale = lax.rsqrt(var + 1e-06)
            rows = pl.ds(pl.multiple_of(base + g * 16, 16), 16)
            for j in range(blocks):
                lanes = pl.ds(j * LANE, LANE)
                value = cols[j] * scale * mod[1:2, lanes] + mod[0:1, lanes]
                xm[rows, lanes] = value.astype(jnp.bfloat16)

    def project(first_col, dst, parts, norm):
        low, count = own_n * parts[0], own_n * len(parts)
        for i in range(inner // qkv_cols):
            cols = pl.ds(first_col + i * qkv_cols, qkv_cols)
            x = xm[low : low + count, :]
            p = jnp.dot(x, wqkv[:, cols], preferred_element_type=jnp.float32)
            for h in range(qkv_cols // HEAD):
                at = (i * qkv_cols + h * HEAD) * (2 if norm is None else 1)
                for part in parts:
                    top = own_n * part - low
                    ph = p[top : top + own_n, h * HEAD : (h + 1) * HEAD]
                    rows = pl.ds(split * part, own_n)
                    if norm is not None:
                        ms = jnp.sum(ph * ph, axis=-1, keepdims=True) * (1.0 / HEAD)
                        ph = ph * (lax.rsqrt(ms + 1e-06) * norm)
                    elif part:
                        ph = ph * allow[...]
                    if norm == 1.0:
                        dst[pl.ds(at, HEAD), rows] = ph.T.astype(jnp.bfloat16)
                    else:
                        dst[rows, pl.ds(at, HEAD)] = ph.astype(jnp.bfloat16)

    def project_query():
        project(0, q_s, (0,), Q_SCALE)

    def project_key(*parts):
        project(inner, k_s, parts, 1.0)

    def project_value(*parts):
        project(2 * inner, v_s, parts, None)

    first_seg = seg == n_seg - 1

    def extract(k, p):
        patch = lax.rem(k + 1, n_seg)

        @pl.loop(p * piece_n, (p + 1) * piece_n)
        def _(f):
            frame = order_ref[patch * FP + f]
            for c in range(tw_len):
                x = tok[frame, c].astype(jnp.float32)
                for j in range(blocks):
                    xt[pl.ds(c * blocks + j, th_len, stride=tw_len * blocks), :] = x[
                        :, j * LANE : (j + 1) * LANE
                    ]
            for r in range(th_len):
                y = xt[pl.ds(r * tw_len * blocks, tw_len * blocks), :]
                ext[k, f, 1 + r, 1 : 1 + tw_len] = y.astype(jnp.bfloat16).reshape(
                    tw_len, blocks, LANE
                )

    def bring(k, p, source=None):
        if source is None:

            @pl.when(first_seg)
            def _():
                extract(k, p)

            @pl.when(jnp.logical_not(first_seg))
            def _():
                next_copy(k, p).wait_recv()

        elif source:
            extract(k, p)
        else:
            next_copy(k, p).wait_recv()

        for d, (da, db) in enumerate(DIRS):

            @pl.when(has(da, db))
            def _():
                halo_copy(k, p, d).start()

    def take_halo(k):
        for d, (da, db) in enumerate(DIRS):

            @pl.when(has(-da, -db))
            def _():
                for p in range(PIECES):
                    halo_copy(k, p, d).wait_recv()

        @pl.loop(0, FP)
        def _(f):
            base = (own_n + f * ring_n) * blocks
            for r in (0, th_len + 1):
                y = ext[k, f, r].reshape(wide * blocks, LANE)
                xs[pl.ds(base, wide * blocks), :] = y.astype(jnp.float32)
                base = base + wide * blocks
            for c in (0, tw_len + 1):
                for r in range(th_len):
                    xs[pl.ds(base, blocks), :] = ext[k, f, 1 + r, c].astype(jnp.float32)
                    base = base + blocks

    def await_weights(k, group):
        @pl.when(k == 0)
        def _():
            for i in range(inner // qkv_cols):
                wq_copy(group * (inner // qkv_cols) + i).wait()

    @pl.when(jnp.logical_not(first_seg))
    def _():
        for i in range(n_qkv):
            wq_copy(i).wait()
        for i in range(n_out):
            wo_copy(i).wait()

    for p in range(PIECES):
        bring(0, p)

    @pl.loop(0, patches)
    def _(k):
        @pl.loop(0, FP)
        def _(f):
            for r in range(th_len):
                y = ext[k, f, 1 + r, 1 : 1 + tw_len]
                base = (f * th_len + r) * tw_len * blocks
                xs[pl.ds(base, tw_len * blocks), :] = y.reshape(tw_len * blocks, LANE).astype(
                    jnp.float32
                )

        modulate(0)

        @pl.when(first_seg)
        def _():
            await_weights(k, 0)
            project_query()
            take_halo(k)

            @pl.when(k < patches - 1)
            def _():
                for p in range(PIECES):
                    bring(k + 1, p, True)

            modulate(own_n)
            await_weights(k, 1)
            project_key(0, 1)
            await_weights(k, 2)
            project_value(0, 1)

        @pl.when(jnp.logical_not(first_seg))
        def _():
            project_query()
            project_key(0)
            project_value(0)
            take_halo(k)
            modulate(own_n)
            project_key(1)

            @pl.when(k < patches - 1)
            def _():
                bring(k + 1, 0, False)

            project_value(1)

            @pl.when(k < patches - 1)
            def _():
                for p in range(1, PIECES):
                    bring(k + 1, p, False)

        for h in range(heads):
            lanes = pl.ds(h * HEAD, HEAD)
            s = lax.dot_general(
                q_s[:, lanes],
                k_s[lanes, :],
                (((1,), (0,)), ((), ())),
                preferred_element_type=jnp.float32,
            )
            e = jnp.exp2(s)
            o = jnp.dot(
                e.astype(jnp.bfloat16),
                v_s[:, pl.ds(2 * h * HEAD, 2 * HEAD)],
                preferred_element_type=jnp.float32,
            )
            att[:, lanes] = (o[:, :HEAD] / o[:, HEAD:]).astype(jnp.bfloat16)

        @pl.when(jnp.logical_and(first_seg, k == 0))
        def _():
            for i in range(n_out):
                wo_copy(i).wait()

        for i in range(n_out):
            acc = jnp.dot(
                att[...], wout[:, pl.ds(i * out_cols, out_cols)], preferred_element_type=jnp.float32
            )
            for j in range(out_cols // LANE):
                block = i * (out_cols // LANE) + j
                rows = pl.ds(block, own_n, stride=blocks)
                gate = mod[2:3, pl.ds(block * LANE, LANE)]
                xs[rows, :] = xs[rows, :] + gate * acc[:, j * LANE : (j + 1) * LANE]

        for p in range(PIECES):

            @pl.loop(p * piece_n, (p + 1) * piece_n)
            def _(f):
                for r in range(th_len):
                    base = (f * th_len + r) * tw_len * blocks
                    y = xs[pl.ds(base, tw_len * blocks), :]
                    outgo[k, f, r] = y.astype(jnp.bfloat16).reshape(tw_len, blocks, LANE)

            @pl.when(seg > 0)
            def _():
                next_copy(k, p).start()

            @pl.when(jnp.logical_and(seg == 0, k < patches - 1))
            def _():
                fin_copy(k, p).start()

    def emit(landed):
        @pl.loop(0, FP)
        def _(f):
            for r in range(th_len if landed else 0):
                y = fin[f, r].reshape(tw_len * blocks, LANE).astype(jnp.float32)
                base = (f * th_len + r) * tw_len * blocks
                xs[pl.ds(base, tw_len * blocks), :] = y
            for c in range(tw_len):
                base = (f * th_len * tw_len + c) * blocks
                for j in range(blocks):
                    out_ref[f, c, :, pl.ds(j * LANE, LANE)] = xs[
                        pl.ds(base + j, th_len, stride=tw_len * blocks), :
                    ].astype(jnp.bfloat16)

    @pl.when(seg == 0)
    def _():
        emit(False)

    @pl.when(seg > 0)
    def _():
        for p in range(PIECES):
            fin_copy(0, p).wait_recv()
        emit(True)

    @pl.loop(0, patches)
    def _(k):
        @pl.when(jnp.logical_or(seg > 0, k < patches - 1))
        def _():
            for p in range(PIECES):
                next_copy(k, p).wait_send()

        for d, (da, db) in enumerate(DIRS):

            @pl.when(has(da, db))
            def _():
                for p in range(PIECES):
                    halo_copy(k, p, d).wait_send()


def solution(mesh):
    n_seg, n_th, n_tw = (mesh.shape[name] for name in ("segment", "th", "tw"))

    def on_device(tokens, frame_order, tile_pattern, qkv_weight, out_weight, modulation):
        frames, th_len, tw_len, width = tokens.shape
        inner = out_weight.shape[1]
        blocks = width // LANE
        own_n = FP * th_len * tw_len
        halo_n = FP * (2 * (tw_len + 2) + 2 * th_len)
        all_n = own_n + halo_n
        assert halo_n == own_n and n_seg * FP == frames
        sizes = (n_seg, n_th, n_tw, th_len, tw_len, width, inner)
        bf16, f32 = jnp.bfloat16, jnp.float32
        smem = pl.BlockSpec(memory_space=pltpu.SMEM)
        hbm = pl.BlockSpec(memory_space=pl.ANY)
        dma = pltpu.SemaphoreType.DMA
        out = pl.pallas_call(
            functools.partial(kernel, sizes),
            out_shape=jax.ShapeDtypeStruct((FP, tw_len, th_len, width), bf16),
            in_specs=[smem, smem, hbm, hbm, hbm, hbm],
            out_specs=pl.BlockSpec(memory_space=pltpu.VMEM),
            scratch_shapes=[
                pltpu.VMEM((width, 3 * inner), bf16),
                pltpu.VMEM((inner, width), bf16),
                pltpu.VMEM((3, width), f32),
                pltpu.VMEM((frames, tw_len, th_len, width), bf16),
                pltpu.VMEM((n_seg, FP, th_len + 2, tw_len + 2, blocks, LANE), bf16),
                pltpu.VMEM((n_seg, FP, th_len, tw_len, blocks, LANE), bf16),
                pltpu.VMEM((FP, th_len, tw_len, blocks, LANE), bf16),
                pltpu.VMEM((all_n * blocks, LANE), f32),
                pltpu.VMEM((th_len * tw_len * blocks, LANE), f32),
                pltpu.VMEM((2 * own_n, width), bf16),
                pltpu.VMEM((own_n, inner), bf16),
                pltpu.VMEM((inner, 2 * key_split(own_n)), bf16),
                pltpu.VMEM((2 * key_split(own_n), 2 * inner), bf16),
                pltpu.VMEM((own_n, inner), bf16),
                pltpu.VMEM((halo_n, LANE), f32),
                dma((3 * inner // 512 + width // 512 + 2,)),
                dma((n_seg, PIECES)),
                dma((n_seg, PIECES, 8)),
                dma((n_seg, PIECES)),
                dma((n_seg, PIECES, 8)),
                dma((PIECES,)),
            ],
            compiler_params=pltpu.CompilerParams(
                collective_id=0, has_side_effects=True, vmem_limit_bytes=60 * 1024 * 1024
            ),
            name="sections",
        )(
            frame_order,
            tile_pattern,
            tokens.transpose(0, 2, 1, 3),
            qkv_weight,
            out_weight,
            modulation.transpose(1, 0, 2),
        )
        return out.transpose(0, 2, 1, 3)

    in_specs = (
        P(None, "th", "tw", None),
        P(),
        P("th", "tw", None),
        P("segment", None, None),
        P("segment", None, None),
        P("segment", None, None),
    )
    out_specs = P("segment", "th", "tw", None)
    return jax.shard_map(
        on_device, mesh=mesh, in_specs=in_specs, out_specs=out_specs, check_vma=False
    )
```

```python
import functools
import math

import jax
import jax.numpy as jnp
from jax import lax
from jax.experimental import pallas as pl
from jax.experimental.pallas import tpu as pltpu
from jax.sharding import PartitionSpec as P

HEAD = 128
LANE = 128
FP = 4
UNROLL = 6
PIECES = 2
Q_SCALE = math.log2(math.e) / math.sqrt(HEAD)
MESH = pl.DeviceIdType.MESH
DIRS = [(i, j) for i in (-1, 0, 1) for j in (-1, 0, 1) if (i, j) != (0, 0)]


def key_split(count):
    return -(-count // LANE) * LANE


def span(step, length):
    if step == 0:
        return (0, length), (1, length)
    if step < 0:
        return (0, 1), (length + 1, 1)
    return (length - 1, 1), (0, 1)


def kernel(
    sizes,
    order_ref,
    pattern_ref,
    tokens_hbm,
    wqkv_hbm,
    wout_hbm,
    mod_hbm,
    out_ref,
    wqkv,
    wout,
    mod,
    tok,
    ext,
    outgo,
    fin,
    xs,
    xt,
    xm,
    q_s,
    k_s,
    v_s,
    att,
    allow,
    wsem,
    own_recv,
    halo_recv,
    own_send,
    halo_send,
    fin_recv,
):
    n_seg, n_th, n_tw, th_len, tw_len, width, inner = sizes
    heads = inner // HEAD
    blocks = width // LANE
    own_n = FP * th_len * tw_len
    ring_n = 2 * (tw_len + 2) + 2 * th_len
    halo_n = FP * ring_n
    patches = n_seg
    split = key_split(own_n)
    seg = lax.axis_index("segment")
    a = lax.axis_index("th")
    b = lax.axis_index("tw")

    qkv_cols = 512
    n_qkv = 3 * inner // qkv_cols
    out_cols = 512
    n_out = width // out_cols

    def wq_copy(i):
        cols = pl.ds(i * qkv_cols, qkv_cols)
        return pltpu.make_async_copy(wqkv_hbm.at[0, :, cols], wqkv.at[:, cols], wsem.at[i])

    def wo_copy(i):
        cols = pl.ds(i * out_cols, out_cols)
        return pltpu.make_async_copy(wout_hbm.at[0, :, cols], wout.at[:, cols], wsem.at[n_qkv + i])

    mod_copy = pltpu.make_async_copy(mod_hbm.at[:, 0], mod, wsem.at[n_qkv + n_out])
    tok_copy = pltpu.make_async_copy(tokens_hbm, tok, wsem.at[n_qkv + n_out + 1])
    mod_copy.start()

    @pl.when(seg == n_seg - 1)
    def _():
        tok_copy.start()

    for i in range(n_qkv):
        wq_copy(i).start()
    for i in range(n_out):
        wo_copy(i).start()

    row_cells = (tw_len + 2, blocks, LANE)
    for edge, at in ((a == 0, 0), (a == n_th - 1, th_len + 1)):

        @pl.when(edge)
        def _():
            @pl.loop(0, patches * FP)
            def _(i):
                ext[i // FP, i % FP, at] = jnp.zeros(row_cells, ext.dtype)

    for edge, at in ((b == 0, 0), (b == n_tw - 1, tw_len + 1)):

        @pl.when(edge)
        def _():
            @pl.loop(0, patches * FP)
            def _(i):
                for r in range(th_len + 2):
                    ext[i // FP, i % FP, r, at] = jnp.zeros((blocks, LANE), ext.dtype)

    barrier = pltpu.get_barrier_semaphore()
    for s in range(1, n_seg):
        other = lax.rem(seg + s, n_seg)
        pl.semaphore_signal(barrier, inc=1, device_id=(other, a, b), device_id_type=MESH)

    def has(da, db):
        ok = None
        for pos, step, count in ((a, da, n_th), (b, db, n_tw)):
            if step == 0:
                continue
            here = pos > 0 if step < 0 else pos < count - 1
            ok = here if ok is None else jnp.logical_and(ok, here)
        return ok

    for da, db in DIRS:

        @pl.when(has(da, db))
        def _():
            pl.semaphore_signal(
                barrier, inc=1, device_id=(seg, a + da, b + db), device_id_type=MESH
            )

    row = lax.broadcasted_iota(jnp.int32, (halo_n, LANE), 0)
    u = row
    for f in range(1, FP):
        u = jnp.where(row >= f * ring_n, row - f * ring_n, u)
    wide = tw_len + 2
    left = 2 * wide
    keep = jnp.zeros((halo_n, LANE), jnp.float32)
    for low, count, i, j in (
        (0, 1, 0, 0),
        (1, tw_len, 0, 1),
        (wide - 1, 1, 0, 2),
        (wide, 1, 2, 0),
        (wide + 1, tw_len, 2, 1),
        (2 * wide - 1, 1, 2, 2),
        (left, th_len, 1, 0),
        (left + th_len, th_len, 1, 2),
    ):
        flag = pattern_ref[0, 0, 3 * i + j].astype(jnp.float32)
        flag = flag * has(i - 1, j - 1).astype(jnp.float32)
        keep = jnp.where((u >= low) & (u < low + count), flag, keep)
    allow[...] = keep
    for h in range(heads):
        lanes = pl.ds((2 * h + 1) * HEAD, HEAD)
        v_s[0:own_n, lanes] = jnp.full(
            (own_n, HEAD), pattern_ref[0, 0, 4].astype(jnp.float32)
        ).astype(v_s.dtype)
        v_s[split : split + halo_n, lanes] = keep.astype(v_s.dtype)
    gap = split - own_n
    for start in (own_n, split + halo_n):
        for i in range(0, 2 * inner, 512):
            v_s[start : start + gap, i : i + 512] = jnp.zeros((gap, 512), v_s.dtype)

    @pl.loop(0, heads)
    def _(h):
        k_s[pl.ds(pl.multiple_of(h * HEAD, HEAD), HEAD), :] = jnp.zeros(
            (HEAD, 2 * split), k_s.dtype
        )

    near_rows = 1 + (a > 0).astype(jnp.int32) + (a < n_th - 1).astype(jnp.int32)
    near_cols = 1 + (b > 0).astype(jnp.int32) + (b < n_tw - 1).astype(jnp.int32)
    pl.semaphore_wait(barrier, n_seg - 2 + near_rows * near_cols)

    mod_copy.wait()
    mod[1:2, :] = 1.0 + mod[1:2, :]

    @pl.when(seg == n_seg - 1)
    def _():
        tok_copy.wait()

    own_rows, own_cols = pl.ds(1, th_len), pl.ds(1, tw_len)

    piece_n = FP // PIECES

    def own_copy(k, p, target, dst, sem):
        return pltpu.make_async_remote_copy(
            src_ref=outgo.at[k, pl.ds(p * piece_n, piece_n)],
            dst_ref=dst,
            send_sem=own_send.at[k, p],
            recv_sem=sem,
            device_id=(target, a, b),
            device_id_type=MESH,
        )

    def next_copy(k, p):
        dst = ext.at[k, pl.ds(p * piece_n, piece_n), own_rows, own_cols]
        return own_copy(k, p, jnp.maximum(seg - 1, 0), dst, own_recv.at[k, p])

    def fin_copy(k, p):
        dst = fin.at[pl.ds(p * piece_n, piece_n)]
        return own_copy(k, p, lax.rem(k + 1, n_seg), dst, fin_recv.at[p])

    def halo_copy(k, p, d):
        da, db = DIRS[d]
        (r0, rn), (rt, _) = span(da, th_len)
        (c0, cn), (ct, _) = span(db, tw_len)
        frames = pl.ds(p * piece_n, piece_n)
        return pltpu.make_async_remote_copy(
            src_ref=ext.at[k, frames, pl.ds(1 + r0, rn), pl.ds(1 + c0, cn)],
            dst_ref=ext.at[k, frames, pl.ds(rt, rn), pl.ds(ct, cn)],
            send_sem=halo_send.at[k, p, d],
            recv_sem=halo_recv.at[k, p, d],
            device_id=(seg, a + da, b + db),
            device_id_type=MESH,
        )

    def modulate(base, count):
        @pl.loop(0, count // 16, unroll=min(UNROLL, count // 16))
        def _(g):
            start = (base + g * 16) * blocks
            cols = [xs[pl.ds(start + j, 16, stride=blocks), :] for j in range(blocks)]
            total = cols[0]
            for j in range(1, blocks):
                total = total + cols[j]
            mean = jnp.sum(total, axis=-1, keepdims=True) * (1.0 / width)
            cols = [c - mean for c in cols]
            total = cols[0] * cols[0]
            for j in range(1, blocks):
                total = total + cols[j] * cols[j]
            var = jnp.sum(total, axis=-1, keepdims=True) * (1.0 / width)
            scale = lax.rsqrt(var + 1e-06)
            rows = pl.ds(pl.multiple_of(base + g * 16, 16), 16)
            for j in range(blocks):
                lanes = pl.ds(j * LANE, LANE)
                value = cols[j] * scale * mod[1:2, lanes] + mod[0:1, lanes]
                xm[rows, lanes] = value.astype(jnp.bfloat16)

    def project(first_col, dst, parts, norm):
        low, count = own_n * parts[0], own_n * len(parts)
        for i in range(inner // qkv_cols):
            cols = pl.ds(first_col + i * qkv_cols, qkv_cols)
            x = xm[low : low + count, :]
            p = jnp.dot(x, wqkv[:, cols], preferred_element_type=jnp.float32)
            for h in range(qkv_cols // HEAD):
                at = (i * qkv_cols + h * HEAD) * (2 if norm is None else 1)
                for part in parts:
                    top = own_n * part - low
                    ph = p[top : top + own_n, h * HEAD : (h + 1) * HEAD]
                    rows = pl.ds(split * part, own_n)
                    if norm is not None:
                        ms = jnp.sum(ph * ph, axis=-1, keepdims=True) * (1.0 / HEAD)
                        ph = ph * (lax.rsqrt(ms + 1e-06) * norm)
                    elif part:
                        ph = ph * allow[...]
                    if norm == 1.0:
                        dst[pl.ds(at, HEAD), rows] = ph.T.astype(jnp.bfloat16)
                    else:
                        dst[rows, pl.ds(at, HEAD)] = ph.astype(jnp.bfloat16)

    def project_query():
        project(0, q_s, (0,), Q_SCALE)

    def project_key(*parts):
        project(inner, k_s, parts, 1.0)

    def project_value(*parts):
        project(2 * inner, v_s, parts, None)

    first_seg = seg == n_seg - 1

    def extract(k, p):
        patch = lax.rem(k + 1, n_seg)

        @pl.loop(p * piece_n, (p + 1) * piece_n)
        def _(f):
            frame = order_ref[patch * FP + f]
            for c in range(tw_len):
                x = tok[frame, c].astype(jnp.float32)
                for j in range(blocks):
                    xt[pl.ds(c * blocks + j, th_len, stride=tw_len * blocks), :] = x[
                        :, j * LANE : (j + 1) * LANE
                    ]
            for r in range(th_len):
                y = xt[pl.ds(r * tw_len * blocks, tw_len * blocks), :]
                ext[k, f, 1 + r, 1 : 1 + tw_len] = y.astype(jnp.bfloat16).reshape(
                    tw_len, blocks, LANE
                )

    def bring(k, p, source=None):
        if source is None:

            @pl.when(first_seg)
            def _():
                extract(k, p)

            @pl.when(jnp.logical_not(first_seg))
            def _():
                next_copy(k, p).wait_recv()

        elif source:
            extract(k, p)
        else:
            next_copy(k, p).wait_recv()

        for d, (da, db) in enumerate(DIRS):

            @pl.when(has(da, db))
            def _():
                halo_copy(k, p, d).start()

    def take_halo(k):
        for p in range(PIECES):
            for d, (da, db) in enumerate(DIRS):

                @pl.when(has(-da, -db))
                def _():
                    halo_copy(k, p, d).wait_recv()

            @pl.loop(p * piece_n, (p + 1) * piece_n)
            def _(f):
                base = (own_n + f * ring_n) * blocks
                for r in (0, th_len + 1):
                    y = ext[k, f, r].reshape(wide * blocks, LANE)
                    xs[pl.ds(base, wide * blocks), :] = y.astype(jnp.float32)
                    base = base + wide * blocks
                for c in (0, tw_len + 1):
                    for r in range(th_len):
                        xs[pl.ds(base, blocks), :] = ext[k, f, 1 + r, c].astype(jnp.float32)
                        base = base + blocks

            rows = halo_n // PIECES
            modulate(own_n + p * rows, rows)

    def await_weights(k, group):
        @pl.when(k == 0)
        def _():
            for i in range(inner // qkv_cols):
                wq_copy(group * (inner // qkv_cols) + i).wait()

    @pl.when(jnp.logical_not(first_seg))
    def _():
        for i in range(n_qkv):
            wq_copy(i).wait()
        for i in range(n_out):
            wo_copy(i).wait()

    for p in range(PIECES):
        bring(0, p)

    @pl.loop(0, patches)
    def _(k):
        @pl.loop(0, FP)
        def _(f):
            for r in range(th_len):
                y = ext[k, f, 1 + r, 1 : 1 + tw_len]
                base = (f * th_len + r) * tw_len * blocks
                xs[pl.ds(base, tw_len * blocks), :] = y.reshape(tw_len * blocks, LANE).astype(
                    jnp.float32
                )

        modulate(0, own_n)

        @pl.when(first_seg)
        def _():
            await_weights(k, 0)
            project_query()
            take_halo(k)

            @pl.when(k < patches - 1)
            def _():
                for p in range(PIECES):
                    bring(k + 1, p, True)

            await_weights(k, 1)
            project_key(0, 1)
            await_weights(k, 2)
            project_value(0, 1)

        @pl.when(jnp.logical_not(first_seg))
        def _():
            project_query()
            project_key(0)
            project_value(0)
            take_halo(k)
            project_key(1)

            @pl.when(k < patches - 1)
            def _():
                bring(k + 1, 0, False)

            project_value(1)

            @pl.when(k < patches - 1)
            def _():
                for p in range(1, PIECES):
                    bring(k + 1, p, False)

        for h in range(heads):
            lanes = pl.ds(h * HEAD, HEAD)
            s = lax.dot_general(
                q_s[:, lanes],
                k_s[lanes, :],
                (((1,), (0,)), ((), ())),
                preferred_element_type=jnp.float32,
            )
            e = jnp.exp2(s)
            o = jnp.dot(
                e.astype(jnp.bfloat16),
                v_s[:, pl.ds(2 * h * HEAD, 2 * HEAD)],
                preferred_element_type=jnp.float32,
            )
            att[:, lanes] = (o[:, :HEAD] / o[:, HEAD:]).astype(jnp.bfloat16)

        @pl.when(jnp.logical_and(first_seg, k == 0))
        def _():
            for i in range(n_out):
                wo_copy(i).wait()

        for i in range(n_out):
            acc = jnp.dot(
                att[...], wout[:, pl.ds(i * out_cols, out_cols)], preferred_element_type=jnp.float32
            )
            for j in range(out_cols // LANE):
                block = i * (out_cols // LANE) + j
                rows = pl.ds(block, own_n, stride=blocks)
                gate = mod[2:3, pl.ds(block * LANE, LANE)]
                xs[rows, :] = xs[rows, :] + gate * acc[:, j * LANE : (j + 1) * LANE]

        for p in range(PIECES):

            @pl.loop(p * piece_n, (p + 1) * piece_n)
            def _(f):
                for r in range(th_len):
                    base = (f * th_len + r) * tw_len * blocks
                    y = xs[pl.ds(base, tw_len * blocks), :]
                    outgo[k, f, r] = y.astype(jnp.bfloat16).reshape(tw_len, blocks, LANE)

            @pl.when(seg > 0)
            def _():
                next_copy(k, p).start()

            @pl.when(jnp.logical_and(seg == 0, k < patches - 1))
            def _():
                fin_copy(k, p).start()

    def emit(landed):
        @pl.loop(0, FP)
        def _(f):
            for r in range(th_len if landed else 0):
                y = fin[f, r].reshape(tw_len * blocks, LANE).astype(jnp.float32)
                base = (f * th_len + r) * tw_len * blocks
                xs[pl.ds(base, tw_len * blocks), :] = y
            for c in range(tw_len):
                base = (f * th_len * tw_len + c) * blocks
                for j in range(blocks):
                    out_ref[f, c, :, pl.ds(j * LANE, LANE)] = xs[
                        pl.ds(base + j, th_len, stride=tw_len * blocks), :
                    ].astype(jnp.bfloat16)

    @pl.when(seg == 0)
    def _():
        emit(False)

    @pl.when(seg > 0)
    def _():
        for p in range(PIECES):
            fin_copy(0, p).wait_recv()
        emit(True)

    @pl.loop(0, patches)
    def _(k):
        @pl.when(jnp.logical_or(seg > 0, k < patches - 1))
        def _():
            for p in range(PIECES):
                next_copy(k, p).wait_send()

        for d, (da, db) in enumerate(DIRS):

            @pl.when(has(da, db))
            def _():
                for p in range(PIECES):
                    halo_copy(k, p, d).wait_send()


def solution(mesh):
    n_seg, n_th, n_tw = (mesh.shape[name] for name in ("segment", "th", "tw"))

    def on_device(tokens, frame_order, tile_pattern, qkv_weight, out_weight, modulation):
        frames, th_len, tw_len, width = tokens.shape
        inner = out_weight.shape[1]
        blocks = width // LANE
        own_n = FP * th_len * tw_len
        halo_n = FP * (2 * (tw_len + 2) + 2 * th_len)
        all_n = own_n + halo_n
        assert halo_n == own_n and n_seg * FP == frames
        sizes = (n_seg, n_th, n_tw, th_len, tw_len, width, inner)
        bf16, f32 = jnp.bfloat16, jnp.float32
        smem = pl.BlockSpec(memory_space=pltpu.SMEM)
        hbm = pl.BlockSpec(memory_space=pl.ANY)
        dma = pltpu.SemaphoreType.DMA
        out = pl.pallas_call(
            functools.partial(kernel, sizes),
            out_shape=jax.ShapeDtypeStruct((FP, tw_len, th_len, width), bf16),
            in_specs=[smem, smem, hbm, hbm, hbm, hbm],
            out_specs=pl.BlockSpec(memory_space=pltpu.VMEM),
            scratch_shapes=[
                pltpu.VMEM((width, 3 * inner), bf16),
                pltpu.VMEM((inner, width), bf16),
                pltpu.VMEM((3, width), f32),
                pltpu.VMEM((frames, tw_len, th_len, width), bf16),
                pltpu.VMEM((n_seg, FP, th_len + 2, tw_len + 2, blocks, LANE), bf16),
                pltpu.VMEM((n_seg, FP, th_len, tw_len, blocks, LANE), bf16),
                pltpu.VMEM((FP, th_len, tw_len, blocks, LANE), bf16),
                pltpu.VMEM((all_n * blocks, LANE), f32),
                pltpu.VMEM((th_len * tw_len * blocks, LANE), f32),
                pltpu.VMEM((2 * own_n, width), bf16),
                pltpu.VMEM((own_n, inner), bf16),
                pltpu.VMEM((inner, 2 * key_split(own_n)), bf16),
                pltpu.VMEM((2 * key_split(own_n), 2 * inner), bf16),
                pltpu.VMEM((own_n, inner), bf16),
                pltpu.VMEM((halo_n, LANE), f32),
                dma((3 * inner // 512 + width // 512 + 2,)),
                dma((n_seg, PIECES)),
                dma((n_seg, PIECES, 8)),
                dma((n_seg, PIECES)),
                dma((n_seg, PIECES, 8)),
                dma((PIECES,)),
            ],
            compiler_params=pltpu.CompilerParams(
                collective_id=0, has_side_effects=True, vmem_limit_bytes=60 * 1024 * 1024
            ),
            name="sections",
        )(
            frame_order,
            tile_pattern,
            tokens.transpose(0, 2, 1, 3),
            qkv_weight,
            out_weight,
            modulation.transpose(1, 0, 2),
        )
        return out.transpose(0, 2, 1, 3)

    in_specs = (
        P(None, "th", "tw", None),
        P(),
        P("th", "tw", None),
        P("segment", None, None),
        P("segment", None, None),
        P("segment", None, None),
    )
    out_specs = P("segment", "th", "tw", None)
    return jax.shard_map(
        on_device, mesh=mesh, in_specs=in_specs, out_specs=out_specs, check_vma=False
    )
```

```python
import functools
import math

import jax
import jax.numpy as jnp
from jax import lax
from jax.experimental import pallas as pl
from jax.experimental.pallas import tpu as pltpu
from jax.sharding import PartitionSpec as P

HEAD = 128
LANE = 128
FP = 4
UNROLL = 6
FRAMES_OF = ((0, 3), (3, 1))
PIECES = len(FRAMES_OF)
Q_SCALE = math.log2(math.e) / math.sqrt(HEAD)
MESH = pl.DeviceIdType.MESH
DIRS = [(i, j) for i in (-1, 0, 1) for j in (-1, 0, 1) if (i, j) != (0, 0)]


def key_split(count):
    return -(-count // LANE) * LANE


def span(step, length):
    if step == 0:
        return (0, length), (1, length)
    if step < 0:
        return (0, 1), (length + 1, 1)
    return (length - 1, 1), (0, 1)


def kernel(
    sizes,
    order_ref,
    pattern_ref,
    tokens_hbm,
    wqkv_hbm,
    wout_hbm,
    mod_hbm,
    out_ref,
    wqkv,
    wout,
    mod,
    tok,
    ext,
    outgo,
    fin,
    xs,
    xt,
    xm,
    q_s,
    k_s,
    v_s,
    att,
    allow,
    wsem,
    own_recv,
    halo_recv,
    own_send,
    halo_send,
    fin_recv,
):
    n_seg, n_th, n_tw, th_len, tw_len, width, inner = sizes
    heads = inner // HEAD
    blocks = width // LANE
    own_n = FP * th_len * tw_len
    ring_n = 2 * (tw_len + 2) + 2 * th_len
    halo_n = FP * ring_n
    patches = n_seg
    split = key_split(own_n)
    seg = lax.axis_index("segment")
    a = lax.axis_index("th")
    b = lax.axis_index("tw")

    qkv_cols = 512
    n_qkv = 3 * inner // qkv_cols
    out_cols = 512
    n_out = width // out_cols

    def wq_copy(i):
        cols = pl.ds(i * qkv_cols, qkv_cols)
        return pltpu.make_async_copy(wqkv_hbm.at[0, :, cols], wqkv.at[:, cols], wsem.at[i])

    def wo_copy(i):
        cols = pl.ds(i * out_cols, out_cols)
        return pltpu.make_async_copy(wout_hbm.at[0, :, cols], wout.at[:, cols], wsem.at[n_qkv + i])

    mod_copy = pltpu.make_async_copy(mod_hbm.at[:, 0], mod, wsem.at[n_qkv + n_out])
    tok_copy = pltpu.make_async_copy(tokens_hbm, tok, wsem.at[n_qkv + n_out + 1])
    mod_copy.start()

    @pl.when(seg == n_seg - 1)
    def _():
        tok_copy.start()

    for i in range(n_qkv):
        wq_copy(i).start()
    for i in range(n_out):
        wo_copy(i).start()

    row_cells = (tw_len + 2, blocks, LANE)
    for edge, at in ((a == 0, 0), (a == n_th - 1, th_len + 1)):

        @pl.when(edge)
        def _():
            @pl.loop(0, patches * FP)
            def _(i):
                ext[i // FP, i % FP, at] = jnp.zeros(row_cells, ext.dtype)

    for edge, at in ((b == 0, 0), (b == n_tw - 1, tw_len + 1)):

        @pl.when(edge)
        def _():
            @pl.loop(0, patches * FP)
            def _(i):
                for r in range(th_len + 2):
                    ext[i // FP, i % FP, r, at] = jnp.zeros((blocks, LANE), ext.dtype)

    barrier = pltpu.get_barrier_semaphore()
    for s in range(1, n_seg):
        other = lax.rem(seg + s, n_seg)
        pl.semaphore_signal(barrier, inc=1, device_id=(other, a, b), device_id_type=MESH)

    def has(da, db):
        ok = None
        for pos, step, count in ((a, da, n_th), (b, db, n_tw)):
            if step == 0:
                continue
            here = pos > 0 if step < 0 else pos < count - 1
            ok = here if ok is None else jnp.logical_and(ok, here)
        return ok

    for da, db in DIRS:

        @pl.when(has(da, db))
        def _():
            pl.semaphore_signal(
                barrier, inc=1, device_id=(seg, a + da, b + db), device_id_type=MESH
            )

    row = lax.broadcasted_iota(jnp.int32, (halo_n, LANE), 0)
    u = row
    for f in range(1, FP):
        u = jnp.where(row >= f * ring_n, row - f * ring_n, u)
    wide = tw_len + 2
    left = 2 * wide
    keep = jnp.zeros((halo_n, LANE), jnp.float32)
    for low, count, i, j in (
        (0, 1, 0, 0),
        (1, tw_len, 0, 1),
        (wide - 1, 1, 0, 2),
        (wide, 1, 2, 0),
        (wide + 1, tw_len, 2, 1),
        (2 * wide - 1, 1, 2, 2),
        (left, th_len, 1, 0),
        (left + th_len, th_len, 1, 2),
    ):
        flag = pattern_ref[0, 0, 3 * i + j].astype(jnp.float32)
        flag = flag * has(i - 1, j - 1).astype(jnp.float32)
        keep = jnp.where((u >= low) & (u < low + count), flag, keep)
    allow[...] = keep
    for h in range(heads):
        lanes = pl.ds((2 * h + 1) * HEAD, HEAD)
        v_s[0:own_n, lanes] = jnp.full(
            (own_n, HEAD), pattern_ref[0, 0, 4].astype(jnp.float32)
        ).astype(v_s.dtype)
        v_s[split : split + halo_n, lanes] = keep.astype(v_s.dtype)
    gap = split - own_n
    for start in (own_n, split + halo_n):
        for i in range(0, 2 * inner, 512):
            v_s[start : start + gap, i : i + 512] = jnp.zeros((gap, 512), v_s.dtype)

    @pl.loop(0, heads)
    def _(h):
        k_s[pl.ds(pl.multiple_of(h * HEAD, HEAD), HEAD), :] = jnp.zeros(
            (HEAD, 2 * split), k_s.dtype
        )

    near_rows = 1 + (a > 0).astype(jnp.int32) + (a < n_th - 1).astype(jnp.int32)
    near_cols = 1 + (b > 0).astype(jnp.int32) + (b < n_tw - 1).astype(jnp.int32)
    pl.semaphore_wait(barrier, n_seg - 2 + near_rows * near_cols)

    mod_copy.wait()
    mod[1:2, :] = 1.0 + mod[1:2, :]

    @pl.when(seg == n_seg - 1)
    def _():
        tok_copy.wait()

    own_rows, own_cols = pl.ds(1, th_len), pl.ds(1, tw_len)

    def own_copy(k, p, target, dst, sem):
        return pltpu.make_async_remote_copy(
            src_ref=outgo.at[k, pl.ds(*FRAMES_OF[p])],
            dst_ref=dst,
            send_sem=own_send.at[k, p],
            recv_sem=sem,
            device_id=(target, a, b),
            device_id_type=MESH,
        )

    def next_copy(k, p):
        dst = ext.at[k, pl.ds(*FRAMES_OF[p]), own_rows, own_cols]
        return own_copy(k, p, jnp.maximum(seg - 1, 0), dst, own_recv.at[k, p])

    def fin_copy(k, p):
        dst = fin.at[pl.ds(*FRAMES_OF[p])]
        return own_copy(k, p, lax.rem(k + 1, n_seg), dst, fin_recv.at[p])

    def halo_copy(k, p, d):
        da, db = DIRS[d]
        (r0, rn), (rt, _) = span(da, th_len)
        (c0, cn), (ct, _) = span(db, tw_len)
        frames = pl.ds(*FRAMES_OF[p])
        return pltpu.make_async_remote_copy(
            src_ref=ext.at[k, frames, pl.ds(1 + r0, rn), pl.ds(1 + c0, cn)],
            dst_ref=ext.at[k, frames, pl.ds(rt, rn), pl.ds(ct, cn)],
            send_sem=halo_send.at[k, p, d],
            recv_sem=halo_recv.at[k, p, d],
            device_id=(seg, a + da, b + db),
            device_id_type=MESH,
        )

    def modulate(base):
        @pl.loop(0, own_n // 16, unroll=UNROLL)
        def _(g):
            start = (base + g * 16) * blocks
            cols = [xs[pl.ds(start + j, 16, stride=blocks), :] for j in range(blocks)]
            total = cols[0]
            for j in range(1, blocks):
                total = total + cols[j]
            mean = jnp.sum(total, axis=-1, keepdims=True) * (1.0 / width)
            cols = [c - mean for c in cols]
            total = cols[0] * cols[0]
            for j in range(1, blocks):
                total = total + cols[j] * cols[j]
            var = jnp.sum(total, axis=-1, keepdims=True) * (1.0 / width)
            scale = lax.rsqrt(var + 1e-06)
            rows = pl.ds(pl.multiple_of(base + g * 16, 16), 16)
            for j in range(blocks):
                lanes = pl.ds(j * LANE, LANE)
                value = cols[j] * scale * mod[1:2, lanes] + mod[0:1, lanes]
                xm[rows, lanes] = value.astype(jnp.bfloat16)

    def project(first_col, dst, parts, norm):
        low, count = own_n * parts[0], own_n * len(parts)
        for i in range(inner // qkv_cols):
            cols = pl.ds(first_col + i * qkv_cols, qkv_cols)
            x = xm[low : low + count, :]
            p = jnp.dot(x, wqkv[:, cols], preferred_element_type=jnp.float32)
            for h in range(qkv_cols // HEAD):
                at = (i * qkv_cols + h * HEAD) * (2 if norm is None else 1)
                for part in parts:
                    top = own_n * part - low
                    ph = p[top : top + own_n, h * HEAD : (h + 1) * HEAD]
                    rows = pl.ds(split * part, own_n)
                    if norm is not None:
                        ms = jnp.sum(ph * ph, axis=-1, keepdims=True) * (1.0 / HEAD)
                        ph = ph * (lax.rsqrt(ms + 1e-06) * norm)
                    elif part:
                        ph = ph * allow[...]
                    if norm == 1.0:
                        dst[pl.ds(at, HEAD), rows] = ph.T.astype(jnp.bfloat16)
                    else:
                        dst[rows, pl.ds(at, HEAD)] = ph.astype(jnp.bfloat16)

    def project_query():
        project(0, q_s, (0,), Q_SCALE)

    def project_key(*parts):
        project(inner, k_s, parts, 1.0)

    def project_value(*parts):
        project(2 * inner, v_s, parts, None)

    first_seg = seg == n_seg - 1

    def extract(k, p):
        patch = lax.rem(k + 1, n_seg)

        @pl.loop(FRAMES_OF[p][0], sum(FRAMES_OF[p]))
        def _(f):
            frame = order_ref[patch * FP + f]
            for c in range(tw_len):
                x = tok[frame, c].astype(jnp.float32)
                for j in range(blocks):
                    xt[pl.ds(c * blocks + j, th_len, stride=tw_len * blocks), :] = x[
                        :, j * LANE : (j + 1) * LANE
                    ]
            for r in range(th_len):
                y = xt[pl.ds(r * tw_len * blocks, tw_len * blocks), :]
                ext[k, f, 1 + r, 1 : 1 + tw_len] = y.astype(jnp.bfloat16).reshape(
                    tw_len, blocks, LANE
                )

    def bring(k, p, source=None):
        if source is None:

            @pl.when(first_seg)
            def _():
                extract(k, p)

            @pl.when(jnp.logical_not(first_seg))
            def _():
                next_copy(k, p).wait_recv()

        elif source:
            extract(k, p)
        else:
            next_copy(k, p).wait_recv()

        for d, (da, db) in enumerate(DIRS):

            @pl.when(has(da, db))
            def _():
                halo_copy(k, p, d).start()

    def take_halo(k):
        for d, (da, db) in enumerate(DIRS):

            @pl.when(has(-da, -db))
            def _():
                for p in range(PIECES):
                    halo_copy(k, p, d).wait_recv()

        @pl.loop(0, FP)
        def _(f):
            base = (own_n + f * ring_n) * blocks
            for r in (0, th_len + 1):
                y = ext[k, f, r].reshape(wide * blocks, LANE)
                xs[pl.ds(base, wide * blocks), :] = y.astype(jnp.float32)
                base = base + wide * blocks
            for c in (0, tw_len + 1):
                for r in range(th_len):
                    xs[pl.ds(base, blocks), :] = ext[k, f, 1 + r, c].astype(jnp.float32)
                    base = base + blocks

    def await_weights(k, group):
        @pl.when(k == 0)
        def _():
            for i in range(inner // qkv_cols):
                wq_copy(group * (inner // qkv_cols) + i).wait()

    @pl.when(jnp.logical_not(first_seg))
    def _():
        for i in range(n_qkv):
            wq_copy(i).wait()
        for i in range(n_out):
            wo_copy(i).wait()

    for p in range(PIECES):
        bring(0, p)

    @pl.loop(0, patches)
    def _(k):
        @pl.loop(0, FP)
        def _(f):
            for r in range(th_len):
                y = ext[k, f, 1 + r, 1 : 1 + tw_len]
                base = (f * th_len + r) * tw_len * blocks
                xs[pl.ds(base, tw_len * blocks), :] = y.reshape(tw_len * blocks, LANE).astype(
                    jnp.float32
                )

        modulate(0)

        @pl.when(first_seg)
        def _():
            await_weights(k, 0)
            project_query()
            take_halo(k)

            @pl.when(k < patches - 1)
            def _():
                for p in range(PIECES):
                    bring(k + 1, p, True)

            modulate(own_n)
            await_weights(k, 1)
            project_key(0, 1)
            await_weights(k, 2)
            project_value(0, 1)

        @pl.when(jnp.logical_not(first_seg))
        def _():
            project_query()
            project_key(0)
            project_value(0)
            take_halo(k)
            modulate(own_n)
            project_key(1)

            @pl.when(k < patches - 1)
            def _():
                bring(k + 1, 0, False)

            project_value(1)

            @pl.when(k < patches - 1)
            def _():
                for p in range(1, PIECES):
                    bring(k + 1, p, False)

        for h in range(heads):
            lanes = pl.ds(h * HEAD, HEAD)
            s = lax.dot_general(
                q_s[:, lanes],
                k_s[lanes, :],
                (((1,), (0,)), ((), ())),
                preferred_element_type=jnp.float32,
            )
            e = jnp.exp2(s)
            o = jnp.dot(
                e.astype(jnp.bfloat16),
                v_s[:, pl.ds(2 * h * HEAD, 2 * HEAD)],
                preferred_element_type=jnp.float32,
            )
            att[:, lanes] = (o[:, :HEAD] / o[:, HEAD:]).astype(jnp.bfloat16)

        @pl.when(jnp.logical_and(first_seg, k == 0))
        def _():
            for i in range(n_out):
                wo_copy(i).wait()

        for i in range(n_out):
            acc = jnp.dot(
                att[...], wout[:, pl.ds(i * out_cols, out_cols)], preferred_element_type=jnp.float32
            )
            for j in range(out_cols // LANE):
                block = i * (out_cols // LANE) + j
                rows = pl.ds(block, own_n, stride=blocks)
                gate = mod[2:3, pl.ds(block * LANE, LANE)]
                xs[rows, :] = xs[rows, :] + gate * acc[:, j * LANE : (j + 1) * LANE]

        for p in range(PIECES):

            @pl.loop(FRAMES_OF[p][0], sum(FRAMES_OF[p]))
            def _(f):
                for r in range(th_len):
                    base = (f * th_len + r) * tw_len * blocks
                    y = xs[pl.ds(base, tw_len * blocks), :]
                    outgo[k, f, r] = y.astype(jnp.bfloat16).reshape(tw_len, blocks, LANE)

            @pl.when(seg > 0)
            def _():
                next_copy(k, p).start()

            @pl.when(jnp.logical_and(seg == 0, k < patches - 1))
            def _():
                fin_copy(k, p).start()

    def emit(landed):
        @pl.loop(0, FP)
        def _(f):
            for r in range(th_len if landed else 0):
                y = fin[f, r].reshape(tw_len * blocks, LANE).astype(jnp.float32)
                base = (f * th_len + r) * tw_len * blocks
                xs[pl.ds(base, tw_len * blocks), :] = y
            for c in range(tw_len):
                base = (f * th_len * tw_len + c) * blocks
                for j in range(blocks):
                    out_ref[f, c, :, pl.ds(j * LANE, LANE)] = xs[
                        pl.ds(base + j, th_len, stride=tw_len * blocks), :
                    ].astype(jnp.bfloat16)

    @pl.when(seg == 0)
    def _():
        emit(False)

    @pl.when(seg > 0)
    def _():
        for p in range(PIECES):
            fin_copy(0, p).wait_recv()
        emit(True)

    @pl.loop(0, patches)
    def _(k):
        @pl.when(jnp.logical_or(seg > 0, k < patches - 1))
        def _():
            for p in range(PIECES):
                next_copy(k, p).wait_send()

        for d, (da, db) in enumerate(DIRS):

            @pl.when(has(da, db))
            def _():
                for p in range(PIECES):
                    halo_copy(k, p, d).wait_send()


def solution(mesh):
    n_seg, n_th, n_tw = (mesh.shape[name] for name in ("segment", "th", "tw"))

    def on_device(tokens, frame_order, tile_pattern, qkv_weight, out_weight, modulation):
        frames, th_len, tw_len, width = tokens.shape
        inner = out_weight.shape[1]
        blocks = width // LANE
        own_n = FP * th_len * tw_len
        halo_n = FP * (2 * (tw_len + 2) + 2 * th_len)
        all_n = own_n + halo_n
        assert halo_n == own_n and n_seg * FP == frames
        sizes = (n_seg, n_th, n_tw, th_len, tw_len, width, inner)
        bf16, f32 = jnp.bfloat16, jnp.float32
        smem = pl.BlockSpec(memory_space=pltpu.SMEM)
        hbm = pl.BlockSpec(memory_space=pl.ANY)
        dma = pltpu.SemaphoreType.DMA
        out = pl.pallas_call(
            functools.partial(kernel, sizes),
            out_shape=jax.ShapeDtypeStruct((FP, tw_len, th_len, width), bf16),
            in_specs=[smem, smem, hbm, hbm, hbm, hbm],
            out_specs=pl.BlockSpec(memory_space=pltpu.VMEM),
            scratch_shapes=[
                pltpu.VMEM((width, 3 * inner), bf16),
                pltpu.VMEM((inner, width), bf16),
                pltpu.VMEM((3, width), f32),
                pltpu.VMEM((frames, tw_len, th_len, width), bf16),
                pltpu.VMEM((n_seg, FP, th_len + 2, tw_len + 2, blocks, LANE), bf16),
                pltpu.VMEM((n_seg, FP, th_len, tw_len, blocks, LANE), bf16),
                pltpu.VMEM((FP, th_len, tw_len, blocks, LANE), bf16),
                pltpu.VMEM((all_n * blocks, LANE), f32),
                pltpu.VMEM((th_len * tw_len * blocks, LANE), f32),
                pltpu.VMEM((2 * own_n, width), bf16),
                pltpu.VMEM((own_n, inner), bf16),
                pltpu.VMEM((inner, 2 * key_split(own_n)), bf16),
                pltpu.VMEM((2 * key_split(own_n), 2 * inner), bf16),
                pltpu.VMEM((own_n, inner), bf16),
                pltpu.VMEM((halo_n, LANE), f32),
                dma((3 * inner // 512 + width // 512 + 2,)),
                dma((n_seg, PIECES)),
                dma((n_seg, PIECES, 8)),
                dma((n_seg, PIECES)),
                dma((n_seg, PIECES, 8)),
                dma((PIECES,)),
            ],
            compiler_params=pltpu.CompilerParams(
                collective_id=0, has_side_effects=True, vmem_limit_bytes=60 * 1024 * 1024
            ),
            name="sections",
        )(
            frame_order,
            tile_pattern,
            tokens.transpose(0, 2, 1, 3),
            qkv_weight,
            out_weight,
            modulation.transpose(1, 0, 2),
        )
        return out.transpose(0, 2, 1, 3)

    in_specs = (
        P(None, "th", "tw", None),
        P(),
        P("th", "tw", None),
        P("segment", None, None),
        P("segment", None, None),
        P("segment", None, None),
    )
    out_specs = P("segment", "th", "tw", None)
    return jax.shard_map(
        on_device, mesh=mesh, in_specs=in_specs, out_specs=out_specs, check_vma=False
    )
```
